32 devices in a mesh: rows: 8 (over y, x, core), cols: 4 (over z).
Axes of the slice: x: 2, y: 2, z: 4, core: 2. Of those that a mesh axis runs over, the one named last changes fastest.
Arguments:
- grads: bfloat16 [9216, 8192], P(('rows', 'cols')), may hold values from -6 to 6
- tests: float32 [64, 8192], P(None, 'cols'), may hold values from -6 to 6
Outputs:
- solution: float32 [64, 8192], P(None, 'cols')
- scores: float32 [64, 9216], P(None, ('rows', 'cols'))
The draws below stay inside these ranges and needn't reach their ends.
All inputs are finite; a program needn't handle non-finite values.
Results may differ from the reference program's by a relative error of at most 0.0041.
Values may be sent and summed in bfloat16 or wider, within the bound.
A program may use at most 64 MiB of HBM per device.

```python
import jax
import jax.numpy as jnp
from jax import lax

K = 8192
TESTS = 64
ITERS = 2
N_TOTAL = 9216


def spiked(array, stream_key, source, target, blocks, factor):
    def block_of(dim):
        return (jnp.arange(array.shape[dim]) // (array.shape[dim] // blocks)).reshape((-1,) + (1,) * (array.ndim - 1 - dim))

    near = jax.random.permutation(stream_key, blocks)[block_of(target)]
    other_side = (block_of(target) + blocks // 2) % blocks
    return jnp.where((block_of(source) == near) | (block_of(source) == other_side), factor * array, array)


def level_of(rng, extent, cuts, low, largest):
    loudness, own = 1.0, jax.random.fold_in(rng, 6)
    for dim, blocks in cuts:
        heights = jnp.exp(jax.random.uniform(jax.random.fold_in(own, dim), (blocks,), jnp.float32, low / len(cuts), largest / len(cuts)))
        loudness = loudness * jnp.repeat(heights, extent[dim] // blocks).reshape([-1 if axis == dim else 1 for axis in range(len(extent))])
    return loudness


def centred(rng, extent, scale, most, shards=(), dtype=jnp.bfloat16):
    result = scale * jax.random.normal(rng, extent, jnp.float32)
    if shards:
        result = result * level_of(rng, extent, shards, -0.22, 0.18)
    return jnp.clip(result, -most, most).astype(dtype)


def noise_with(rng, extent, deviation, limit, split, heavy, held_as=jnp.bfloat16):
    array = deviation * jax.random.normal(rng, extent, jnp.float32)
    if split:
        array = array * level_of(rng, extent, split, -0.22, 0.18)
    return jnp.clip(spiked(array, jax.random.fold_in(rng, 3), *heavy), -limit, limit).astype(held_as)


def setup_inputs(seed: int = 0) -> dict:
    seeds = jax.random.split(jax.random.key(seed), 3)
    grads = noise_with(seeds[0], (N_TOTAL, K), 1.0, 6.0, ((0, 32),), (0, 1, 32, 2.75))
    tests = centred(seeds[1], (TESTS, K), 1.0, 6.0, ((1, 4),), jnp.float32)
    return {"grads": grads, "tests": tests}


damping = 0.5


def reference(grads, tests):
    n_total = grads.shape[0]
    width = grads.shape[1]
    solution = jnp.zeros(tests.shape, jnp.float32)
    residual = tests
    direction = tests
    norm_now = jnp.sum(residual * residual, axis=1)
    for step in range(ITERS):
        dir_bf = direction.astype(jnp.bfloat16)
        proj = lax.dot_general(grads, dir_bf, (((1,), (1,)), ((), ())), preferred_element_type=jnp.float32).astype(jnp.bfloat16)
        back = lax.dot_general(proj, grads, (((0,), (0,)), ((), ())), preferred_element_type=jnp.float32)
        image = back / n_total + damping * direction
        curv = jnp.sum(direction * image, axis=1)
        alpha = norm_now / curv
        solution = solution + alpha[:, None] * direction
        residual = residual - alpha[:, None] * image
        norm_next = jnp.sum(residual * residual, axis=1)
        direction = residual + (norm_next / norm_now)[:, None] * direction
        norm_now = norm_next
    sol_bf = solution.astype(jnp.bfloat16)
    scores = lax.dot_general(sol_bf, grads, (((1,), (1,)), ((), ())), preferred_element_type=jnp.float32)
    return solution, scores * (width ** -0.5)
```

```python
import functools

import jax
import jax.numpy as jnp
from jax import lax
from jax.experimental import pallas as pl
from jax.experimental.pallas import tpu as pltpu
from jax.sharding import PartitionSpec as P

MESH = pl.DeviceIdType.MESH
GROUPS = 2

damping = 0.5


def plain(grads, tests):
    n_total = grads.shape[0] * lax.axis_size("rows") * lax.axis_size("cols")
    width = grads.shape[1]
    own = tests.shape[1]
    direction = lax.all_gather(tests, "cols", axis=1, tiled=True)
    norm_now = jnp.sum(direction * direction, axis=1)

    def project(d):
        return lax.dot_general(
            grads, d.astype(jnp.bfloat16), (((1,), (1,)), ((), ())), preferred_element_type=jnp.float32
        )

    partial_value = lax.dot_general(
        project(direction).astype(jnp.bfloat16), grads, (((0,), (0,)), ((), ())), preferred_element_type=jnp.float32
    )
    image = lax.psum(partial_value, ("rows", "cols")) / n_total + damping * direction
    alpha = norm_now / jnp.sum(direction * image, axis=1)
    solution = alpha[:, None] * direction
    residual = direction - alpha[:, None] * image
    norm_next = jnp.sum(residual * residual, axis=1)
    direction = residual + (norm_next / norm_now)[:, None] * direction
    proj = project(direction)
    curv = lax.psum(jnp.sum(proj * proj.astype(jnp.bfloat16).astype(jnp.float32), axis=0), ("rows", "cols"))
    curv = curv / n_total + damping * jnp.sum(direction * direction, axis=1)
    solution = solution + (norm_next / curv)[:, None] * direction
    scores = lax.dot_general(
        solution.astype(jnp.bfloat16), grads, (((1,), (1,)), ((), ())), preferred_element_type=jnp.float32
    )
    mine = lax.dynamic_slice_in_dim(solution, lax.axis_index("cols") * own, own, axis=1)
    return (mine, scores * width ** (-0.5))


def flip(value, mask):
    out, b = value, 1
    while b <= mask:
        if mask & b:
            out = out + (1 - 2 * lax.rem(lax.div(value, b), 2)) * b
        b *= 2
    return out


def kernel(
    nr, nc, grads, tests, out, scores, g, tz, tb, bk, keep, box, r, ro, px, p1s, mail, near,
    load_sem, gsend, grecv, tsend, trecv, xsend, xrecv, osend, orecv, nsend, nrecv, msend, mrecv, bsend, brecv, asend, arecv,
):
    row, col = lax.axis_index("rows"), lax.axis_index("cols")
    core, xy = lax.rem(row, 2), lax.div(row, 2)
    quad = nr // 2
    count, own = tests.shape
    held, width = grads.shape
    half = own // 2
    share = half // quad
    chips = quad * nc
    n_total = held * nr * nc
    span = count // GROUPS
    away = sorted(range(1, nc), reverse=True)
    groups = range(GROUPS)

    def rows(a):
        return pl.ds(a * span, span)

    def at(index, size):
        return pl.ds(pl.multiple_of(index * size, size), size)

    def peer(dxy, dz):
        return {"rows": flip(xy, dxy) * 2 + core, "cols": flip(col, dz)}

    twin = {"rows": xy * 2 + 1 - core, "cols": col}
    others = [(dxy, dz) for dz in away + [0] for dxy in range(quad - 1, -1, -1) if dxy or dz]
    sent = []

    def remote(src, dst, send, recv, device):
        copy = pltpu.make_async_remote_copy(
            src_ref=src, dst_ref=dst, send_sem=send, recv_sem=recv, device_id=device, device_id_type=MESH
        )
        copy.start()
        sent.append(copy)
        return copy

    mine = pltpu.make_async_copy(tests, tz, load_sem.at[nc])
    mine.start()
    loads = []
    for dz in range(nc):
        loads.append(
            pltpu.make_async_copy(
                grads.at[:, at(flip(col, dz) * 2 + core, half)],
                g.at[at(core, held), pl.ds(dz * half, half)],
                load_sem.at[dz],
            )
        )
        loads[-1].start()

    barrier = pltpu.get_barrier_semaphore()
    greet = [twin] + [peer(dxy, 0) for dxy in range(1, quad)] + [peer(0, dz) for dz in range(1, nc)]
    for device in greet:
        pl.semaphore_signal(barrier, inc=1, device_id=device, device_id_type=MESH)
    mine.wait()
    for a in groups:
        tb[a, 0] = tz[rows(a), at(core, half)].astype(jnp.bfloat16)
    pl.semaphore_wait(barrier, len(greet))

    arriving = {}
    for a in groups:
        for dz in away:
            arriving[a, dz] = remote(tb.at[a, 0], tb.at[a, dz], tsend.at[a, dz], trecv.at[a, dz], peer(0, dz))
    for dz in range(nc):
        arriving[dz] = remote(
            grads.at[:, at(flip(col, dz) * 2 + 1 - core, half)],
            g.at[at(core, held), pl.ds(dz * half, half)],
            gsend.at[dz],
            grecv.at[dz],
            twin,
        )

    def across(x):
        return jnp.sum(x, axis=1, keepdims=True)

    diagonal = lax.broadcasted_iota(jnp.int32, (span, 128), 0) == lax.broadcasted_iota(jnp.int32, (span, 128), 1)
    line = lax.broadcasted_iota(jnp.int32, (8, 128), 0)

    def pack(columns):
        tile = jnp.zeros((8, 128), jnp.float32)
        for i, c in enumerate(columns):
            flat = jnp.sum(jnp.where(diagonal, jnp.broadcast_to(c, (span, 128)), 0.0), axis=0, keepdims=True)
            tile = jnp.where(line == i, jnp.broadcast_to(flat, (8, 128)), tile)
        return tile

    def unpack(tile, i):
        return across(jnp.where(diagonal, jnp.broadcast_to(tile[i : i + 1, :], (span, 128)), 0.0))

    def project(block, dz):
        return lax.dot_general(
            block, g[:, pl.ds(dz * half, half)], (((1,), (1,)), ((), ())), preferred_element_type=jnp.float32
        )

    def exchange(k, a, value):
        px[k, a, 0] = value
        return remote(px.at[k, a, 0], px.at[k, a, 1], xsend.at[k, a], xrecv.at[k, a], twin)

    def post(k, a, tile):
        mail[k, a, 0] = tile
        for dxy, dz in others:
            j = dz * quad + dxy
            arriving["mail", k, a, j] = remote(
                mail.at[k, a, 0], mail.at[k, a, j], msend.at[k, a, j], mrecv.at[k, a, j], peer(dxy, dz)
            )

    def collect(k, a):
        tile = mail[k, a, 0]
        for j in range(1, chips):
            arriving["mail", k, a, j].wait_recv()
            tile = tile + mail[k, a, j]
        return tile

    squares = [across(tz[rows(a), :] * tz[rows(a), :]) for a in groups]
    ready = set()

    for a in groups:
        total = jnp.zeros((span, 2 * held), jnp.float32)
        for dz in range(nc):
            if dz not in ready:
                loads[dz].wait()
                arriving[dz].wait_recv()
                ready.add(dz)
            if dz:
                arriving[a, dz].wait_recv()
            total = total + project(tb[a, dz], dz)
        exchange(0, a, total).wait_recv()
        p1 = px[0, a, 0] + px[0, a, 1]
        p1s[a] = p1
        post(0, a, pack([across(p1 * p1), squares[a]]))
        flat = p1.astype(jnp.bfloat16)
        for dz in away + [0]:
            back = jnp.dot(flat, g[:, pl.ds(dz * half, half)], preferred_element_type=jnp.float32)
            bk[a, dz] = back.astype(jnp.bfloat16)
            if dz == 0:
                keep[a] = back
            for dxy in range(quad):
                if dxy or dz:
                    j = dz * quad + dxy
                    arriving["back", a, j] = remote(
                        bk.at[a, dz, :, at(flip(xy, dxy), share)],
                        box.at[a, j],
                        bsend.at[a, j],
                        brecv.at[a, j],
                        peer(dxy, dz),
                    )

    alphas, norms = [], []
    for a in groups:
        tile = collect(0, a)
        first, rr = unpack(tile, 0), unpack(tile, 1) * (1.0 / quad)
        alpha = rr / (first * (1.0 / n_total) + damping * rr)
        alphas.append(alpha)
        norms.append((first, rr))
        total = keep[a, :, at(xy, share)]
        for j in range(1, chips):
            arriving["back", a, j].wait_recv()
            total = total + box[a, j].astype(jnp.float32)
        t = tz[rows(a), at(core * quad + xy, share)]
        res = t - alpha * (total * (1.0 / n_total) + damping * t)
        r[a, 0, :, at(xy, share)] = res.astype(jnp.bfloat16)
        for dxy, dz in others:
            j = dz * quad + dxy
            arriving["res", a, j] = remote(
                r.at[a, 0, :, at(xy, share)], r.at[a, dz, :, at(xy, share)], asend.at[a, j], arecv.at[a, j], peer(dxy, dz)
            )
        near[a, 0] = pack([across(res * res), across(res * t)])
        arriving["near", a] = remote(near.at[a, 0], near.at[a, 1], nsend.at[a], nrecv.at[a], twin)

    seconds = []
    for a in groups:
        total = jnp.zeros((span, 2 * held), jnp.float32)
        for dz in range(nc):
            for dxy in range(quad):
                if dxy or dz:
                    arriving["res", a, dz * quad + dxy].wait_recv()
            if dz == 0:
                arriving["other", a] = remote(r.at[a, 0], ro.at[a], osend.at[a], orecv.at[a], twin)
            total = total + project(r[a, dz], dz)
        exchange(1, a, total).wait_recv()
        p2 = px[1, a, 0] + px[1, a, 1]
        p1 = p1s[a]
        arriving["near", a].wait_recv()
        tile = near[a, 0] + near[a, 1]
        moved = pack([jnp.zeros((span, 1), jnp.float32)] * 2 + [across(p2 * p2), across(p2 * p1)])
        post(1, a, tile + moved)
        seconds.append(p2)

    for a in groups:
        alpha, (first, rr), p2, p1 = alphas[a], norms[a], seconds[a], p1s[a]
        tile = collect(1, a)
        rn, rt, ss, sp = [unpack(tile, i) for i in range(4)]
        beta = rn / rr
        curv = (ss + 2.0 * beta * sp + beta * beta * first) * (1.0 / n_total)
        curv = curv + damping * (rn + 2.0 * beta * rt + beta * beta * rr)
        step = rn / curv
        keepers = alpha + step * beta
        out[rows(a), at(core, half)] = keepers * tz[rows(a), at(core, half)] + step * r[a, 0].astype(jnp.float32)
        arriving["other", a].wait_recv()
        out[rows(a), at(1 - core, half)] = keepers * tz[rows(a), at(1 - core, half)] + step * ro[a].astype(jnp.float32)
        both = (keepers * p1 + step * p2) * width ** (-0.5)
        scores[rows(a), :] = jnp.where(core == 0, both[:, :held], both[:, held:])
    for copy in sent:
        copy.wait_send()


def per_device(nr, nc, grads, tests):
    count, own = tests.shape
    held, width = grads.shape
    quad = nr // 2
    chips = quad * nc
    half = own // 2
    span = count // GROUPS
    power = nr & (nr - 1) == 0 and nc & (nc - 1) == 0 and nr >= 4 and nc >= 2
    if not power or own * nc != width or half % (128 * quad) or count % (16 * GROUPS) or span > 128 or held % 16 or held * width > 2**23:
        return plain(grads, tests)
    bf16, f32 = jnp.bfloat16, jnp.float32
    dma = pltpu.SemaphoreType.DMA
    return pl.pallas_call(
        functools.partial(kernel, nr, nc),
        out_shape=(
            jax.ShapeDtypeStruct((count, own), f32),
            jax.ShapeDtypeStruct((count, held), f32),
        ),
        in_specs=[pl.BlockSpec(memory_space=pl.ANY)] * 2,
        out_specs=[pl.BlockSpec(memory_space=pltpu.VMEM)] * 2,
        scratch_shapes=[
            pltpu.VMEM((2 * held, nc * half), bf16),
            pltpu.VMEM((count, own), f32),
            pltpu.VMEM((GROUPS, nc, span, half), bf16),
            pltpu.VMEM((GROUPS, nc, span, half), bf16),
            pltpu.VMEM((GROUPS, span, half), f32),
            pltpu.VMEM((GROUPS, chips, span, half // quad), bf16),
            pltpu.VMEM((GROUPS, nc, span, half), bf16),
            pltpu.VMEM((GROUPS, span, half), bf16),
            pltpu.VMEM((2, GROUPS, 2, span, 2 * held), f32),
            pltpu.VMEM((GROUPS, span, 2 * held), f32),
            pltpu.VMEM((2, GROUPS, chips, 8, 128), f32),
            pltpu.VMEM((GROUPS, 2, 8, 128), f32),
            dma((nc + 1,)),
            dma((nc,)),
            dma((nc,)),
            dma((GROUPS, nc)),
            dma((GROUPS, nc)),
            dma((2, GROUPS)),
            dma((2, GROUPS)),
            dma((GROUPS,)),
            dma((GROUPS,)),
            dma((GROUPS,)),
            dma((GROUPS,)),
            dma((2, GROUPS, chips)),
            dma((2, GROUPS, chips)),
            dma((GROUPS, chips)),
            dma((GROUPS, chips)),
            dma((GROUPS, chips)),
            dma((GROUPS, chips)),
        ],
        compiler_params=pltpu.CompilerParams(collective_id=0, has_side_effects=True, vmem_limit_bytes=48 * 2**20),
    )(grads, tests)


def solution(mesh):
    placed = (P(("rows", "cols"), None), P(None, "cols"))
    return jax.shard_map(
        functools.partial(per_device, mesh.shape["rows"], mesh.shape["cols"]),
        mesh=mesh,
        in_specs=placed,
        out_specs=(P(None, "cols"), P(None, ("rows", "cols"))),
        check_vma=False,
    )
```

```python
import functools

import jax
import jax.numpy as jnp
from jax import lax
from jax.experimental import pallas as pl
from jax.experimental.pallas import tpu as pltpu
from jax.sharding import PartitionSpec as P

MESH = pl.DeviceIdType.MESH
GROUPS = 2

damping = 0.5


def plain(grads, tests):
    n_total = grads.shape[0] * lax.axis_size("rows") * lax.axis_size("cols")
    width = grads.shape[1]
    own = tests.shape[1]
    direction = lax.all_gather(tests, "cols", axis=1, tiled=True)
    norm_now = jnp.sum(direction * direction, axis=1)

    def project(d):
        return lax.dot_general(
            grads, d.astype(jnp.bfloat16), (((1,), (1,)), ((), ())), preferred_element_type=jnp.float32
        )

    partial_value = lax.dot_general(
        project(direction).astype(jnp.bfloat16), grads, (((0,), (0,)), ((), ())), preferred_element_type=jnp.float32
    )
    image = lax.psum(partial_value, ("rows", "cols")) / n_total + damping * direction
    alpha = norm_now / jnp.sum(direction * image, axis=1)
    solution = alpha[:, None] * direction
    residual = direction - alpha[:, None] * image
    norm_next = jnp.sum(residual * residual, axis=1)
    direction = residual + (norm_next / norm_now)[:, None] * direction
    proj = project(direction)
    curv = lax.psum(jnp.sum(proj * proj.astype(jnp.bfloat16).astype(jnp.float32), axis=0), ("rows", "cols"))
    curv = curv / n_total + damping * jnp.sum(direction * direction, axis=1)
    solution = solution + (norm_next / curv)[:, None] * direction
    scores = lax.dot_general(
        solution.astype(jnp.bfloat16), grads, (((1,), (1,)), ((), ())), preferred_element_type=jnp.float32
    )
    mine = lax.dynamic_slice_in_dim(solution, lax.axis_index("cols") * own, own, axis=1)
    return (mine, scores * width ** (-0.5))


def flip(value, mask):
    out, b = value, 1
    while b <= mask:
        if mask & b:
            out = out + (1 - 2 * lax.rem(lax.div(value, b), 2)) * b
        b *= 2
    return out


def kernel(
    nr, nc, grads, tests, out, scores, g, tz, tb, bk, keep, box, r, ro, px, p1s, mail, near,
    load_sem, gsend, grecv, tsend, trecv, xsend, xrecv, osend, orecv, nsend, nrecv, msend, mrecv, bsend, brecv, asend, arecv,
):
    row, col = lax.axis_index("rows"), lax.axis_index("cols")
    core, xy = lax.rem(row, 2), lax.div(row, 2)
    quad = nr // 2
    count, own = tests.shape
    held, width = grads.shape
    half = own // 2
    share = half // quad
    chips = quad * nc
    n_total = held * nr * nc
    span = count // GROUPS
    away = sorted(range(1, nc), reverse=True)
    groups = range(GROUPS)

    def rows(a):
        return pl.ds(a * span, span)

    def at(index, size):
        return pl.ds(pl.multiple_of(index * size, size), size)

    def peer(dxy, dz):
        return {"rows": flip(xy, dxy) * 2 + core, "cols": flip(col, dz)}

    twin = {"rows": xy * 2 + 1 - core, "cols": col}
    others = [(dxy, dz) for dz in away + [0] for dxy in range(quad - 1, -1, -1) if dxy or dz]
    sent = []

    def remote(src, dst, send, recv, device):
        copy = pltpu.make_async_remote_copy(
            src_ref=src, dst_ref=dst, send_sem=send, recv_sem=recv, device_id=device, device_id_type=MESH
        )
        copy.start()
        sent.append(copy)
        return copy

    mine = pltpu.make_async_copy(tests, tz, load_sem.at[nc])
    mine.start()
    loads = []
    for dz in range(nc):
        loads.append(
            pltpu.make_async_copy(
                grads.at[:, at(flip(col, dz) * 2 + core, half)],
                g.at[at(core, held), pl.ds(dz * half, half)],
                load_sem.at[dz],
            )
        )
        loads[-1].start()

    barrier = pltpu.get_barrier_semaphore()
    greet = [twin] + [peer(dxy, 0) for dxy in range(1, quad)] + [peer(0, dz) for dz in range(1, nc)]
    for device in greet:
        pl.semaphore_signal(barrier, inc=1, device_id=device, device_id_type=MESH)
    mine.wait()
    for a in groups:
        tb[a, 0] = tz[rows(a), at(core, half)].astype(jnp.bfloat16)
    pl.semaphore_wait(barrier, len(greet))

    arriving = {}
    for a in groups:
        for dz in away:
            arriving[a, dz] = remote(tb.at[a, 0], tb.at[a, dz], tsend.at[a, dz], trecv.at[a, dz], peer(0, dz))
    for dz in range(nc):
        arriving[dz] = remote(
            grads.at[:, at(flip(col, dz) * 2 + 1 - core, half)],
            g.at[at(core, held), pl.ds(dz * half, half)],
            gsend.at[dz],
            grecv.at[dz],
            twin,
        )

    def across(x):
        return jnp.sum(x, axis=1, keepdims=True)

    diagonal = lax.broadcasted_iota(jnp.int32, (span, 128), 0) == lax.broadcasted_iota(jnp.int32, (span, 128), 1)
    line = lax.broadcasted_iota(jnp.int32, (8, 128), 0)

    def pack(columns):
        tile = jnp.zeros((8, 128), jnp.float32)
        for i, c in enumerate(columns):
            flat = jnp.sum(jnp.where(diagonal, jnp.broadcast_to(c, (span, 128)), 0.0), axis=0, keepdims=True)
            tile = jnp.where(line == i, jnp.broadcast_to(flat, (8, 128)), tile)
        return tile

    def unpack(tile, i):
        return across(jnp.where(diagonal, jnp.broadcast_to(tile[i : i + 1, :], (span, 128)), 0.0))

    def project(block, dz):
        return lax.dot_general(
            block, g[:, pl.ds(dz * half, half)], (((1,), (1,)), ((), ())), preferred_element_type=jnp.float32
        )

    def exchange(k, a, value):
        px[k, a, 0] = value
        return remote(px.at[k, a, 0], px.at[k, a, 1], xsend.at[k, a], xrecv.at[k, a], twin)

    def post(k, a, tile):
        mail[k, a, 0] = tile
        for dxy, dz in others:
            j = dz * quad + dxy
            arriving["mail", k, a, j] = remote(
                mail.at[k, a, 0], mail.at[k, a, j], msend.at[k, a, j], mrecv.at[k, a, j], peer(dxy, dz)
            )

    def collect(k, a):
        tile = mail[k, a, 0]
        for j in range(1, chips):
            arriving["mail", k, a, j].wait_recv()
            tile = tile + mail[k, a, j]
        return tile

    squares = [across(tz[rows(a), :] * tz[rows(a), :]) for a in groups]
    ready = set()

    for a in groups:
        total = jnp.zeros((span, 2 * held), jnp.float32)
        for dz in range(nc):
            if dz not in ready:
                loads[dz].wait()
                arriving[dz].wait_recv()
                ready.add(dz)
            if dz:
                arriving[a, dz].wait_recv()
            total = total + project(tb[a, dz], dz)
        exchange(0, a, total).wait_recv()
        p1 = px[0, a, 0] + px[0, a, 1]
        p1s[a] = p1
        post(0, a, pack([across(p1 * p1), squares[a]]))
        flat = p1.astype(jnp.bfloat16)
        for dz in away + [0]:
            back = jnp.dot(flat, g[:, pl.ds(dz * half, half)], preferred_element_type=jnp.float32)
            bk[a, dz] = back.astype(jnp.bfloat16)
            if dz == 0:
                keep[a] = back
            for dxy in range(quad):
                if dxy or dz:
                    j = dz * quad + dxy
                    arriving["back", a, j] = remote(
                        bk.at[a, dz, :, at(flip(xy, dxy), share)],
                        box.at[a, j],
                        bsend.at[a, j],
                        brecv.at[a, j],
                        peer(dxy, dz),
                    )

    alphas, norms = [], []
    for a in groups:
        tile = collect(0, a)
        first, rr = unpack(tile, 0), unpack(tile, 1) * (1.0 / quad)
        alpha = rr / (first * (1.0 / n_total) + damping * rr)
        alphas.append(alpha)
        norms.append((first, rr))
        total = keep[a, :, at(xy, share)]
        for j in range(1, chips):
            arriving["back", a, j].wait_recv()
            total = total + box[a, j].astype(jnp.float32)
        t = tz[rows(a), at(core * quad + xy, share)]
        res = t - alpha * (total * (1.0 / n_total) + damping * t)
        r[a, 0, :, at(xy, share)] = res.astype(jnp.bfloat16)
        for dxy, dz in others:
            j = dz * quad + dxy
            arriving["res", a, j] = remote(
                r.at[a, 0, :, at(xy, share)], r.at[a, dz, :, at(xy, share)], asend.at[a, j], arecv.at[a, j], peer(dxy, dz)
            )
        near[a, 0] = pack([across(res * res), across(res * t)])
        arriving["near", a] = remote(near.at[a, 0], near.at[a, 1], nsend.at[a], nrecv.at[a], twin)

    seconds = []
    for a in groups:
        total = jnp.zeros((span, 2 * held), jnp.float32)
        for dz in range(nc):
            for dxy in range(quad):
                if dxy or dz:
                    arriving["res", a, dz * quad + dxy].wait_recv()
            if dz == 0:
                arriving["other", a] = remote(r.at[a, 0], ro.at[a], osend.at[a], orecv.at[a], twin)
            total = total + project(r[a, dz], dz)
        exchange(1, a, total).wait_recv()
        p2 = px[1, a, 0] + px[1, a, 1]
        p1 = p1s[a]
        arriving["near", a].wait_recv()
        tile = near[a, 0] + near[a, 1]
        moved = pack([jnp.zeros((span, 1), jnp.float32)] * 2 + [across(p2 * p2), across(p2 * p1)])
        post(1, a, tile + moved)
        seconds.append(p2)

    for a in groups:
        alpha, (first, rr), p2, p1 = alphas[a], norms[a], seconds[a], p1s[a]
        tile = collect(1, a)
        rn, rt, ss, sp = [unpack(tile, i) for i in range(4)]
        beta = rn / rr
        curv = (ss + 2.0 * beta * sp + beta * beta * first) * (1.0 / n_total)
        curv = curv + damping * (rn + 2.0 * beta * rt + beta * beta * rr)
        step = rn / curv
        keepers = alpha + step * beta
        out[rows(a), at(core, half)] = keepers * tz[rows(a), at(core, half)] + step * r[a, 0].astype(jnp.float32)
        arriving["other", a].wait_recv()
        out[rows(a), at(1 - core, half)] = keepers * tz[rows(a), at(1 - core, half)] + step * ro[a].astype(jnp.float32)
        both = (keepers * p1 + step * p2) * width ** (-0.5)
        scores[rows(a), :] = jnp.where(core == 0, both[:, :held], both[:, held:])
    for copy in sent:
        copy.wait_send()


def per_device(nr, nc, grads, tests):
    count, own = tests.shape
    held, width = grads.shape
    quad = nr // 2
    chips = quad * nc
    half = own // 2
    span = count // GROUPS
    power = nr & (nr - 1) == 0 and nc & (nc - 1) == 0 and nr >= 4 and nc >= 2
    if not power or own * nc != width or half % (128 * quad) or count % (16 * GROUPS) or span > 128 or held % 16 or held * width > 2**23:
        return plain(grads, tests)
    bf16, f32 = jnp.bfloat16, jnp.float32
    dma = pltpu.SemaphoreType.DMA
    return pl.pallas_call(
        functools.partial(kernel, nr, nc),
        out_shape=(
            jax.ShapeDtypeStruct((count, own), f32),
            jax.ShapeDtypeStruct((count, held), f32),
        ),
        in_specs=[pl.BlockSpec(memory_space=pltpu.HBM)] * 2,
        out_specs=[pl.BlockSpec(memory_space=pltpu.VMEM)] * 2,
        scratch_shapes=[
            pltpu.VMEM((2 * held, nc * half), bf16),
            pltpu.VMEM((count, own), f32),
            pltpu.VMEM((GROUPS, nc, span, half), bf16),
            pltpu.VMEM((GROUPS, nc, span, half), bf16),
            pltpu.VMEM((GROUPS, span, half), f32),
            pltpu.VMEM((GROUPS, chips, span, half // quad), bf16),
            pltpu.VMEM((GROUPS, nc, span, half), bf16),
            pltpu.VMEM((GROUPS, span, half), bf16),
            pltpu.VMEM((2, GROUPS, 2, span, 2 * held), f32),
            pltpu.VMEM((GROUPS, span, 2 * held), f32),
            pltpu.VMEM((2, GROUPS, chips, 8, 128), f32),
            pltpu.VMEM((GROUPS, 2, 8, 128), f32),
            dma((nc + 1,)),
            dma((nc,)),
            dma((nc,)),
            dma((GROUPS, nc)),
            dma((GROUPS, nc)),
            dma((2, GROUPS)),
            dma((2, GROUPS)),
            dma((GROUPS,)),
            dma((GROUPS,)),
            dma((GROUPS,)),
            dma((GROUPS,)),
            dma((2, GROUPS, chips)),
            dma((2, GROUPS, chips)),
            dma((GROUPS, chips)),
            dma((GROUPS, chips)),
            dma((GROUPS, chips)),
            dma((GROUPS, chips)),
        ],
        compiler_params=pltpu.CompilerParams(collective_id=0, has_side_effects=True, vmem_limit_bytes=53 * 2**20),
    )(grads, tests)


def solution(mesh):
    placed = (P(("rows", "cols"), None), P(None, "cols"))
    return jax.shard_map(
        functools.partial(per_device, mesh.shape["rows"], mesh.shape["cols"]),
        mesh=mesh,
        in_specs=placed,
        out_specs=(P(None, "cols"), P(None, ("rows", "cols"))),
        check_vma=False,
    )
```

```python
import functools

import jax
import jax.numpy as jnp
from jax import lax
from jax.experimental import pallas as pl
from jax.experimental.pallas import tpu as pltpu
from jax.sharding import PartitionSpec as P

MESH = pl.DeviceIdType.MESH
GROUPS = 2

damping = 0.5


def plain(grads, tests):
    n_total = grads.shape[0] * lax.axis_size("rows") * lax.axis_size("cols")
    width = grads.shape[1]
    own = tests.shape[1]
    direction = lax.all_gather(tests, "cols", axis=1, tiled=True)
    norm_now = jnp.sum(direction * direction, axis=1)

    def project(d):
        return lax.dot_general(
            grads, d.astype(jnp.bfloat16), (((1,), (1,)), ((), ())), preferred_element_type=jnp.float32
        )

    partial_value = lax.dot_general(
        project(direction).astype(jnp.bfloat16), grads, (((0,), (0,)), ((), ())), preferred_element_type=jnp.float32
    )
    image = lax.psum(partial_value, ("rows", "cols")) / n_total + damping * direction
    alpha = norm_now / jnp.sum(direction * image, axis=1)
    solution = alpha[:, None] * direction
    residual = direction - alpha[:, None] * image
    norm_next = jnp.sum(residual * residual, axis=1)
    direction = residual + (norm_next / norm_now)[:, None] * direction
    proj = project(direction)
    curv = lax.psum(jnp.sum(proj * proj.astype(jnp.bfloat16).astype(jnp.float32), axis=0), ("rows", "cols"))
    curv = curv / n_total + damping * jnp.sum(direction * direction, axis=1)
    solution = solution + (norm_next / curv)[:, None] * direction
    scores = lax.dot_general(
        solution.astype(jnp.bfloat16), grads, (((1,), (1,)), ((), ())), preferred_element_type=jnp.float32
    )
    mine = lax.dynamic_slice_in_dim(solution, lax.axis_index("cols") * own, own, axis=1)
    return (mine, scores * width ** (-0.5))


def flip(value, mask):
    out, b = value, 1
    while b <= mask:
        if mask & b:
            out = out + (1 - 2 * lax.rem(lax.div(value, b), 2)) * b
        b *= 2
    return out


def kernel(
    nr, nc, grads, tests, out, scores, g, tz, tb, bk, keep, relay, late, box, r, ro, px, p1s, mail, near,
    load_sem, gsend, grecv, tsend, trecv, fsend, frecv, xsend, xrecv, osend, orecv, msend, mrecv, bsend, brecv,
    csend, crecv, dsend, drecv, asend, arecv, usend, urecv, vsend, vrecv,
):
    row, col = lax.axis_index("rows"), lax.axis_index("cols")
    core, xy = lax.rem(row, 2), lax.div(row, 2)
    quad = nr // 2
    count, own = tests.shape
    held, width = grads.shape
    half = own // 2
    share = half // quad
    chips = quad * nc
    n_total = held * nr * nc
    span = count // GROUPS
    away = sorted(range(1, nc), reverse=True)
    groups = range(GROUPS)
    A, B = groups

    def rows(a):
        return pl.ds(a * span, span)

    def at(index, size):
        return pl.ds(pl.multiple_of(index * size, size), size)

    def peer(dxy, dz):
        return {"rows": flip(xy, dxy) * 2 + core, "cols": flip(col, dz)}

    twin = {"rows": xy * 2 + 1 - core, "cols": col}
    everyone = [(dxy, dz) for dz in away + [0] for dxy in range(quad - 1, -1, -1) if dxy or dz]
    sent = []
    flying = {}

    def remote(src, dst, send, recv, device):
        copy = pltpu.make_async_remote_copy(
            src_ref=src, dst_ref=dst, send_sem=send, recv_sem=recv, device_id=device, device_id_type=MESH
        )
        copy.start()
        sent.append(copy)
        return copy

    mine = pltpu.make_async_copy(tests, tz, load_sem.at[nc])
    mine.start()
    loads = []
    for dz in range(nc):
        loads.append(
            pltpu.make_async_copy(
                grads.at[:, at(flip(col, dz) * 2 + core, half)],
                g.at[at(core, held), pl.ds(dz * half, half)],
                load_sem.at[dz],
            )
        )
        loads[-1].start()

    barrier = pltpu.get_barrier_semaphore()
    greet = [twin] + [peer(dxy, 0) for dxy in range(1, quad)] + [peer(0, dz) for dz in range(1, nc)]
    for device in greet:
        pl.semaphore_signal(barrier, inc=1, device_id=device, device_id_type=MESH)
    mine.wait()
    for a in groups:
        tb[a, 0] = tz[rows(a), at(core, half)].astype(jnp.bfloat16)
    pl.semaphore_wait(barrier, len(greet))

    here = at(xy, share)
    for dz in away:
        part = tb.at[B, 0, :, here]
        flying["quarter", dz] = remote(part, tb.at[B, dz, :, here], tsend.at[B, dz], trecv.at[B, dz], peer(0, dz))
    for dz in away:
        flying["tests", dz] = remote(tb.at[A, 0], tb.at[A, dz], tsend.at[A, dz], trecv.at[A, dz], peer(0, dz))
    for dz in range(nc):
        flying["grads", dz] = remote(
            grads.at[:, at(flip(col, dz) * 2 + 1 - core, half)],
            g.at[at(core, held), pl.ds(dz * half, half)],
            gsend.at[dz],
            grecv.at[dz],
            twin,
        )

    def across(x):
        return jnp.sum(x, axis=1, keepdims=True)

    diagonal = lax.broadcasted_iota(jnp.int32, (count, 128), 0) == lax.broadcasted_iota(jnp.int32, (count, 128), 1)
    line = lax.broadcasted_iota(jnp.int32, (8, 128), 0)

    def pack(columns):
        tile = jnp.zeros((8, 128), jnp.float32)
        for i, c in enumerate(columns):
            if c is not None:
                flat = jnp.sum(jnp.where(diagonal, jnp.broadcast_to(c, (count, 128)), 0.0), axis=0, keepdims=True)
                tile = jnp.where(line == i, jnp.broadcast_to(flat, (8, 128)), tile)
        return tile

    def unpack(tile, i):
        return across(jnp.where(diagonal, jnp.broadcast_to(tile[i : i + 1, :], (count, 128)), 0.0))

    def project(block, lo, size):
        return lax.dot_general(
            block, g[:, pl.ds(lo, size)], (((1,), (1,)), ((), ())), preferred_element_type=jnp.float32
        )

    def slot(buf, a, dz):
        return project(buf[a, dz], dz * half, half)

    def piece(buf, a, dz, dxy):
        at_xy = flip(xy, dxy)
        return project(buf[a, dz, :, at(at_xy, share)], pl.multiple_of(dz * half + at_xy * share, share), share)

    def exchange(k, a, value):
        px[k, a, 0] = value
        return remote(px.at[k, a, 0], px.at[k, a, 1], xsend.at[k, a], xrecv.at[k, a], twin)

    def post(k, tile):
        mail[k, 0] = tile
        for dxy, dz in everyone:
            j = dz * quad + dxy
            flying["mail", k, j] = remote(mail.at[k, 0], mail.at[k, j], msend.at[k, j], mrecv.at[k, j], peer(dxy, dz))

    def collect(k):
        tile = mail[k, 0]
        for j in range(1, chips):
            flying["mail", k, j].wait_recv()
            tile = tile + mail[k, j]
        return tile

    squares = across(tz[...] * tz[...])
    for dz in range(nc):
        loads[dz].wait()
        flying["grads", dz].wait_recv()
    totals = [slot(tb, a, 0) for a in groups]
    for dz in away:
        flying["quarter", dz].wait_recv()
    for dxy in range(quad - 1, 0, -1):
        part = tb.at[B, pl.ds(1, nc - 1), :, here]
        flying["spread", dxy] = remote(part, part, fsend.at[dxy], frecv.at[dxy], peer(dxy, 0))
    for dz in range(1, nc):
        totals[B] = totals[B] + piece(tb, B, dz, 0)
    for dz in range(1, nc):
        flying["tests", dz].wait_recv()
        totals[A] = totals[A] + slot(tb, A, dz)
    flying["first", A] = exchange(0, A, totals[A])
    for dxy in range(1, quad):
        flying["spread", dxy].wait_recv()
        for dz in range(1, nc):
            totals[B] = totals[B] + piece(tb, B, dz, dxy)
    flying["first", B] = exchange(0, B, totals[B])

    def arrived(k, a, name):
        flying[name, a].wait_recv()
        return px[k, a, 0] + px[k, a, 1]

    def spread(flat, a, dz):
        back = jnp.dot(flat, g[:, pl.ds(dz * half, half)], preferred_element_type=jnp.float32)
        bk[a, dz] = back.astype(jnp.bfloat16)
        return back

    p1s[A] = arrived(0, A, "first")
    flat = p1s[A].astype(jnp.bfloat16)
    for dz in range(nc):
        keep[dz] = spread(flat, A, dz)
    for dxy in range(quad - 1, 0, -1):
        there = at(flip(xy, dxy), share)
        flying["side", dxy] = remote(bk.at[A, :, :, there], relay.at[dxy], csend.at[dxy], crecv.at[dxy], peer(dxy, 0))

    p1s[B] = arrived(0, B, "first")
    flat = p1s[B].astype(jnp.bfloat16)
    for dz in away + [0]:
        back = spread(flat, B, dz)
        if dz == 0:
            keep[nc] = back
        for dxy in range(quad - 1, -1, -1):
            if dxy or dz:
                j = dz * quad + dxy
                flying["back", j] = remote(
                    bk.at[B, dz, :, at(flip(xy, dxy), share)], box.at[j], bsend.at[j], brecv.at[j], peer(dxy, dz)
                )
    post(0, pack([jnp.concatenate([across(p1s[a] * p1s[a]) for a in groups], axis=0), squares]))

    for dxy in range(1, quad):
        flying["side", dxy].wait_recv()
    for dz in away + [0]:
        total = keep[dz, :, here]
        for dxy in range(1, quad):
            total = total + relay[dxy, dz].astype(jnp.float32)
        late[0, dz] = total
        if dz:
            flying["along", dz] = remote(late.at[0, dz], late.at[1, dz], dsend.at[dz], drecv.at[dz], peer(0, dz))
    tile = collect(0)
    first, rr = unpack(tile, 0), unpack(tile, 1) * (1.0 / quad)
    alpha = rr / (first * (1.0 / n_total) + damping * rr)

    def residual(a, total):
        t = tz[rows(a), at(core * quad + xy, share)]
        res = t - alpha[a * span : (a + 1) * span] * (total * (1.0 / n_total) + damping * t)
        r[a, 0, :, here] = res.astype(jnp.bfloat16)
        return across(res * res), across(res * t)

    total = late[0, 0]
    for dz in range(1, nc):
        flying["along", dz].wait_recv()
        total = total + late[1, dz]
    own_sums = [residual(A, total)]
    for dz in away:
        flying["up", dz] = remote(r.at[A, 0, :, here], r.at[A, dz, :, here], usend.at[dz], urecv.at[dz], peer(0, dz))
    total = keep[nc, :, here]
    for j in range(1, chips):
        flying["back", j].wait_recv()
        total = total + box[j].astype(jnp.float32)
    own_sums.append(residual(B, total))
    for dxy, dz in everyone:
        j = dz * quad + dxy
        flying["res", j] = remote(r.at[B, 0, :, here], r.at[B, dz, :, here], asend.at[j], arecv.at[j], peer(dxy, dz))
    near[0] = pack([jnp.concatenate([s[i] for s in own_sums], axis=0) for i in range(2)])
    flying["near"] = remote(near.at[0], near.at[1], osend.at[0], orecv.at[0], twin)

    totals = [piece(r, A, 0, 0), jnp.zeros((span, 2 * held), jnp.float32)]
    for dz in away:
        flying["up", dz].wait_recv()
    for dxy in range(quad - 1, 0, -1):
        part = r.at[A, :, :, here]
        flying["out", dxy] = remote(part, part, vsend.at[dxy], vrecv.at[dxy], peer(dxy, 0))
    for dz in range(1, nc):
        totals[A] = totals[A] + piece(r, A, dz, 0)

    def take(dz):
        for dxy in range(quad):
            if dxy or dz:
                flying["res", dz * quad + dxy].wait_recv()
        totals[B] = totals[B] + slot(r, B, dz)

    take(0)
    take(1)
    for dxy in range(1, quad):
        flying["out", dxy].wait_recv()
        for dz in range(nc):
            totals[A] = totals[A] + piece(r, A, dz, dxy)
    flying["second", A] = exchange(1, A, totals[A])
    for dz in range(2, nc):
        take(dz)
    flying["second", B] = exchange(1, B, totals[B])
    flying["other"] = remote(r.at[:, 0], ro, osend.at[1], orecv.at[1], twin)
    flying["near"].wait_recv()
    tile = near[0] + near[1]
    p2s = [arrived(1, a, "second") for a in groups]
    moved = [jnp.concatenate([across(p2s[a] * other) for a, other in pairs], axis=0) for pairs in (
        [(a, p2s[a]) for a in groups],
        [(a, p1s[a]) for a in groups],
    )]
    post(1, tile + pack([None, None] + moved))

    tile = collect(1)
    rn, rt, ss, sp = [unpack(tile, i) for i in range(4)]
    beta = rn / rr
    curv = (ss + 2.0 * beta * sp + beta * beta * first) * (1.0 / n_total)
    curv = curv + damping * (rn + 2.0 * beta * rt + beta * beta * rr)
    step = rn / curv
    weight = alpha + step * beta
    flying["other"].wait_recv()
    for a in groups:
        w, s = weight[a * span : (a + 1) * span], step[a * span : (a + 1) * span]
        out[rows(a), at(core, half)] = w * tz[rows(a), at(core, half)] + s * r[a, 0].astype(jnp.float32)
        out[rows(a), at(1 - core, half)] = w * tz[rows(a), at(1 - core, half)] + s * ro[a].astype(jnp.float32)
        both = (w * p1s[a] + s * p2s[a]) * width ** (-0.5)
        scores[rows(a), :] = jnp.where(core == 0, both[:, :held], both[:, held:])
    for copy in sent:
        copy.wait_send()


def per_device(nr, nc, grads, tests):
    count, own = tests.shape
    held, width = grads.shape
    quad = nr // 2
    chips = quad * nc
    half = own // 2
    share = half // quad
    span = count // GROUPS
    power = nr & (nr - 1) == 0 and nc & (nc - 1) == 0 and nr >= 4 and nc >= 2
    if not power or own * nc != width or half % (128 * quad) or count % (16 * GROUPS) or count > 128 or held % 16 or held * width > 2**23:
        return plain(grads, tests)
    bf16, f32 = jnp.bfloat16, jnp.float32
    dma = pltpu.SemaphoreType.DMA
    pairs = [(nc,), (GROUPS, nc), (quad,), (2, GROUPS), (2,), (2, chips), (chips,), (quad,), (nc,), (chips,), (nc,), (quad,)]
    return pl.pallas_call(
        functools.partial(kernel, nr, nc),
        out_shape=(
            jax.ShapeDtypeStruct((count, own), f32),
            jax.ShapeDtypeStruct((count, held), f32),
        ),
        in_specs=[pl.BlockSpec(memory_space=pltpu.HBM)] * 2,
        out_specs=[pl.BlockSpec(memory_space=pltpu.VMEM)] * 2,
        scratch_shapes=[
            pltpu.VMEM((2 * held, nc * half), bf16),
            pltpu.VMEM((count, own), f32),
            pltpu.VMEM((GROUPS, nc, span, half), bf16),
            pltpu.VMEM((GROUPS, nc, span, half), bf16),
            pltpu.VMEM((nc + 1, span, half), f32),
            pltpu.VMEM((quad, nc, span, share), bf16),
            pltpu.VMEM((2, nc, span, share), f32),
            pltpu.VMEM((chips, span, share), bf16),
            pltpu.VMEM((GROUPS, nc, span, half), bf16),
            pltpu.VMEM((GROUPS, span, half), bf16),
            pltpu.VMEM((2, GROUPS, 2, span, 2 * held), f32),
            pltpu.VMEM((GROUPS, span, 2 * held), f32),
            pltpu.VMEM((2, chips, 8, 128), f32),
            pltpu.VMEM((2, 8, 128), f32),
            dma((nc + 1,)),
        ]
        + [dma(shape) for shape in pairs for _ in range(2)],
        compiler_params=pltpu.CompilerParams(collective_id=0, has_side_effects=True, vmem_limit_bytes=53 * 2**20),
    )(grads, tests)


def solution(mesh):
    placed = (P(("rows", "cols"), None), P(None, "cols"))
    return jax.shard_map(
        functools.partial(per_device, mesh.shape["rows"], mesh.shape["cols"]),
        mesh=mesh,
        in_specs=placed,
        out_specs=(P(None, "cols"), P(None, ("rows", "cols"))),
        check_vma=False,
    )
```

```python
import functools

import jax
import jax.numpy as jnp
from jax import lax
from jax.experimental import pallas as pl
from jax.experimental.pallas import tpu as pltpu
from jax.sharding import PartitionSpec as P

MESH = pl.DeviceIdType.MESH
GROUPS = 2

damping = 0.5


def plain(grads, tests):
    n_total = grads.shape[0] * lax.axis_size("rows") * lax.axis_size("cols")
    width = grads.shape[1]
    own = tests.shape[1]
    direction = lax.all_gather(tests, "cols", axis=1, tiled=True)
    norm_now = jnp.sum(direction * direction, axis=1)

    def project(d):
        return lax.dot_general(
            grads, d.astype(jnp.bfloat16), (((1,), (1,)), ((), ())), preferred_element_type=jnp.float32
        )

    partial_value = lax.dot_general(
        project(direction).astype(jnp.bfloat16), grads, (((0,), (0,)), ((), ())), preferred_element_type=jnp.float32
    )
    image = lax.psum(partial_value, ("rows", "cols")) / n_total + damping * direction
    alpha = norm_now / jnp.sum(direction * image, axis=1)
    solution = alpha[:, None] * direction
    residual = direction - alpha[:, None] * image
    norm_next = jnp.sum(residual * residual, axis=1)
    direction = residual + (norm_next / norm_now)[:, None] * direction
    proj = project(direction)
    curv = lax.psum(jnp.sum(proj * proj.astype(jnp.bfloat16).astype(jnp.float32), axis=0), ("rows", "cols"))
    curv = curv / n_total + damping * jnp.sum(direction * direction, axis=1)
    solution = solution + (norm_next / curv)[:, None] * direction
    scores = lax.dot_general(
        solution.astype(jnp.bfloat16), grads, (((1,), (1,)), ((), ())), preferred_element_type=jnp.float32
    )
    mine = lax.dynamic_slice_in_dim(solution, lax.axis_index("cols") * own, own, axis=1)
    return (mine, scores * width ** (-0.5))


def flip(value, mask):
    out, b = value, 1
    while b <= mask:
        if mask & b:
            out = out + (1 - 2 * lax.rem(lax.div(value, b), 2)) * b
        b *= 2
    return out


def kernel(
    nr, nc, grads, tests, out, scores, g, tz, tb, bk, keep, relay, late, box, r, ro, px, p1s, mail, near,
    load_sem, gsend, grecv, tsend, trecv, fsend, frecv, xsend, xrecv, osend, orecv, msend, mrecv, bsend, brecv,
    csend, crecv, dsend, drecv, asend, arecv, usend, urecv, vsend, vrecv,
):
    row, col = lax.axis_index("rows"), lax.axis_index("cols")
    core, xy = lax.rem(row, 2), lax.div(row, 2)
    quad = nr // 2
    count, own = tests.shape
    held, width = grads.shape
    half = own // 2
    share = half // quad
    chips = quad * nc
    n_total = held * nr * nc
    span = count // GROUPS
    away = sorted(range(1, nc), reverse=True)
    groups = range(GROUPS)
    A, B = groups

    def rows(a):
        return pl.ds(a * span, span)

    def at(index, size):
        return pl.ds(pl.multiple_of(index * size, size), size)

    def peer(dxy, dz):
        return {"rows": flip(xy, dxy) * 2 + core, "cols": flip(col, dz)}

    twin = {"rows": xy * 2 + 1 - core, "cols": col}
    everyone = [(dxy, dz) for dz in away + [0] for dxy in range(quad - 1, -1, -1) if dxy or dz]
    sent = []
    flying = {}

    def remote(src, dst, send, recv, device):
        copy = pltpu.make_async_remote_copy(
            src_ref=src, dst_ref=dst, send_sem=send, recv_sem=recv, device_id=device, device_id_type=MESH
        )
        copy.start()
        sent.append(copy)
        return copy

    mine = pltpu.make_async_copy(tests, tz, load_sem.at[nc])
    mine.start()
    loads = []
    for dz in range(nc):
        loads.append(
            pltpu.make_async_copy(
                grads.at[:, at(flip(col, dz) * 2 + core, half)],
                g.at[at(core, held), pl.ds(dz * half, half)],
                load_sem.at[dz],
            )
        )
        loads[-1].start()

    barrier = pltpu.get_barrier_semaphore()
    greet = [twin] + [peer(dxy, 0) for dxy in range(1, quad)] + [peer(0, dz) for dz in range(1, nc)]
    for device in greet:
        pl.semaphore_signal(barrier, inc=1, device_id=device, device_id_type=MESH)
    mine.wait()
    for a in groups:
        tb[a, 0] = tz[rows(a), at(core, half)].astype(jnp.bfloat16)
    pl.semaphore_wait(barrier, len(greet))

    here = at(xy, share)
    for dz in away:
        part = tb.at[B, 0, :, here]
        flying["quarter", dz] = remote(part, tb.at[B, dz, :, here], tsend.at[B, dz], trecv.at[B, dz], peer(0, dz))
    for dz in away:
        flying["tests", dz] = remote(tb.at[A, 0], tb.at[A, dz], tsend.at[A, dz], trecv.at[A, dz], peer(0, dz))
    for dz in range(nc):
        flying["grads", dz] = remote(
            grads.at[:, at(flip(col, dz) * 2 + 1 - core, half)],
            g.at[at(core, held), pl.ds(dz * half, half)],
            gsend.at[dz],
            grecv.at[dz],
            twin,
        )

    def across(x):
        return jnp.sum(x, axis=1, keepdims=True)

    diagonal = lax.broadcasted_iota(jnp.int32, (count, 128), 0) == lax.broadcasted_iota(jnp.int32, (count, 128), 1)
    line = lax.broadcasted_iota(jnp.int32, (8, 128), 0)

    def pack(columns):
        tile = jnp.zeros((8, 128), jnp.float32)
        for i, c in enumerate(columns):
            if c is not None:
                flat = jnp.sum(jnp.where(diagonal, jnp.broadcast_to(c, (count, 128)), 0.0), axis=0, keepdims=True)
                tile = jnp.where(line == i, jnp.broadcast_to(flat, (8, 128)), tile)
        return tile

    def unpack(tile, i):
        return across(jnp.where(diagonal, jnp.broadcast_to(tile[i : i + 1, :], (count, 128)), 0.0))

    def project(block, lo, size):
        return lax.dot_general(
            block, g[:, pl.ds(lo, size)], (((1,), (1,)), ((), ())), preferred_element_type=jnp.float32
        )

    def slot(buf, a, dz):
        return project(buf[a, dz], dz * half, half)

    def piece(buf, a, dz, dxy):
        at_xy = flip(xy, dxy)
        return project(buf[a, dz, :, at(at_xy, share)], pl.multiple_of(dz * half + at_xy * share, share), share)

    def exchange(k, a, value):
        px[k, a, 0] = value
        return remote(px.at[k, a, 0], px.at[k, a, 1], xsend.at[k, a], xrecv.at[k, a], twin)

    def post(k, tile):
        mail[k, 0] = tile
        for dxy, dz in everyone:
            j = dz * quad + dxy
            flying["mail", k, j] = remote(mail.at[k, 0], mail.at[k, j], msend.at[k, j], mrecv.at[k, j], peer(dxy, dz))

    def collect(k):
        tile = mail[k, 0]
        for j in range(1, chips):
            flying["mail", k, j].wait_recv()
            tile = tile + mail[k, j]
        return tile

    squares = across(tz[...] * tz[...])
    for dz in range(nc):
        loads[dz].wait()
        flying["grads", dz].wait_recv()
    totals = [slot(tb, a, 0) for a in groups]
    for dz in away:
        flying["quarter", dz].wait_recv()
    for dxy in range(quad - 1, 0, -1):
        part = tb.at[B, pl.ds(1, nc - 1), :, here]
        flying["spread", dxy] = remote(part, part, fsend.at[dxy], frecv.at[dxy], peer(dxy, 0))
    for dz in range(1, nc):
        totals[B] = totals[B] + piece(tb, B, dz, 0)
    for dz in range(1, nc):
        flying["tests", dz].wait_recv()
        totals[A] = totals[A] + slot(tb, A, dz)
    flying["first", A] = exchange(0, A, totals[A])
    for dxy in range(1, quad):
        flying["spread", dxy].wait_recv()
        for dz in range(1, nc):
            totals[B] = totals[B] + piece(tb, B, dz, dxy)
    flying["first", B] = exchange(0, B, totals[B])

    def arrived(k, a, name):
        flying[name, a].wait_recv()
        return px[k, a, 0] + px[k, a, 1]

    def spread(flat, a, dz):
        back = jnp.dot(flat, g[:, pl.ds(dz * half, half)], preferred_element_type=jnp.float32)
        bk[a, dz] = back.astype(jnp.bfloat16)
        return back

    p1s[A] = arrived(0, A, "first")
    flat = p1s[A].astype(jnp.bfloat16)
    for k, lo in enumerate((nc // 2, 0)):
        two = pl.ds(lo, nc // 2)
        for dz in range(lo, lo + nc // 2):
            keep[dz] = spread(flat, A, dz)
        for dxy in range(quad - 1, 0, -1):
            part = bk.at[A, two, :, at(flip(xy, dxy), share)]
            flying["side", k, dxy] = remote(
                part, relay.at[dxy, two], csend.at[k, dxy], crecv.at[k, dxy], peer(dxy, 0)
            )

    p1s[B] = arrived(0, B, "first")
    post(0, pack([jnp.concatenate([across(p1s[a] * p1s[a]) for a in groups], axis=0), squares]))
    flat = p1s[B].astype(jnp.bfloat16)
    for dz in away + [0]:
        back = spread(flat, B, dz)
        if dz == 0:
            keep[nc] = back
        for dxy in range(quad - 1, -1, -1):
            if dxy or dz:
                j = dz * quad + dxy
                flying["back", j] = remote(
                    bk.at[B, dz, :, at(flip(xy, dxy), share)], box.at[j], bsend.at[j], brecv.at[j], peer(dxy, dz)
                )

    for dz in away + [0]:
        total = keep[dz, :, here]
        for dxy in range(1, quad):
            if dz % (nc // 2) == nc // 2 - 1:
                flying["side", 1 - dz // (nc // 2), dxy].wait_recv()
            total = total + relay[dxy, dz].astype(jnp.float32)
        late[0, dz] = total
        if dz:
            flying["along", dz] = remote(late.at[0, dz], late.at[1, dz], dsend.at[dz], drecv.at[dz], peer(0, dz))
    tile = collect(0)
    first, rr = unpack(tile, 0), unpack(tile, 1) * (1.0 / quad)
    alpha = rr / (first * (1.0 / n_total) + damping * rr)

    def residual(a, total):
        t = tz[rows(a), at(core * quad + xy, share)]
        res = t - alpha[a * span : (a + 1) * span] * (total * (1.0 / n_total) + damping * t)
        r[a, 0, :, here] = res.astype(jnp.bfloat16)
        return across(res * res), across(res * t)

    total = keep[nc, :, here]
    for j in range(1, chips):
        flying["back", j].wait_recv()
        total = total + box[j].astype(jnp.float32)
    sums_b = residual(B, total)
    for dz in away:
        flying["up", dz] = remote(r.at[B, 0, :, here], r.at[B, dz, :, here], usend.at[dz], urecv.at[dz], peer(0, dz))
    total = late[0, 0]
    for dz in range(1, nc):
        flying["along", dz].wait_recv()
        total = total + late[1, dz].astype(jnp.float32)
    sums_a = residual(A, total)
    for dxy, dz in everyone:
        j = dz * quad + dxy
        flying["res", j] = remote(r.at[A, 0, :, here], r.at[A, dz, :, here], asend.at[j], arecv.at[j], peer(dxy, dz))
    near[0] = pack([jnp.concatenate([sums_a[i], sums_b[i]], axis=0) for i in range(2)])
    flying["near"] = remote(near.at[0], near.at[1], osend.at[0], orecv.at[0], twin)

    for k, lo in enumerate((0, nc // 2)):
        for dz in range(max(lo, 1), lo + nc // 2):
            flying["up", dz].wait_recv()
        for dxy in range(quad - 1, 0, -1):
            part = r.at[B, pl.ds(lo, nc // 2), :, here]
            flying["out", k, dxy] = remote(part, part, vsend.at[k, dxy], vrecv.at[k, dxy], peer(dxy, 0))

    p2 = jnp.zeros((count, 2 * held), jnp.float32)
    for dz in range(nc):
        for dxy in range(quad):
            if dxy and dz % (nc // 2) == 0:
                flying["out", dz // (nc // 2), dxy].wait_recv()
            if dxy or dz:
                flying["res", dz * quad + dxy].wait_recv()
        p2 = p2 + project(jnp.concatenate([r[a, dz] for a in groups], axis=0), dz * half, half)
    for a in groups:
        px[1, a, 0] = p2[a * span : (a + 1) * span]
    flying["second"] = remote(px.at[1, :, 0], px.at[1, :, 1], xsend.at[1, 0], xrecv.at[1, 0], twin)
    flying["other"] = remote(r.at[:, 0], ro, osend.at[1], orecv.at[1], twin)
    flying["near"].wait_recv()
    tile = near[0] + near[1]
    flying["second"].wait_recv()
    p2s = [px[1, a, 0] + px[1, a, 1] for a in groups]
    moved = [jnp.concatenate([across(p2s[a] * other) for a, other in pairs], axis=0) for pairs in (
        [(a, p2s[a]) for a in groups],
        [(a, p1s[a]) for a in groups],
    )]
    post(1, tile + pack([None, None] + moved))

    tile = collect(1)
    rn, rt, ss, sp = [unpack(tile, i) for i in range(4)]
    beta = rn / rr
    curv = (ss + 2.0 * beta * sp + beta * beta * first) * (1.0 / n_total)
    curv = curv + damping * (rn + 2.0 * beta * rt + beta * beta * rr)
    step = rn / curv
    weight = alpha + step * beta
    flying["other"].wait_recv()
    for a in groups:
        w, s = weight[a * span : (a + 1) * span], step[a * span : (a + 1) * span]
        out[rows(a), at(core, half)] = w * tz[rows(a), at(core, half)] + s * r[a, 0].astype(jnp.float32)
        out[rows(a), at(1 - core, half)] = w * tz[rows(a), at(1 - core, half)] + s * ro[a].astype(jnp.float32)
        both = (w * p1s[a] + s * p2s[a]) * width ** (-0.5)
        scores[rows(a), :] = jnp.where(core == 0, both[:, :held], both[:, held:])
    for copy in sent:
        copy.wait_send()


def store(out, scores, to_out, to_scores, sem):
    copies = [pltpu.make_async_copy(src, dst, sem.at[i]) for i, (src, dst) in enumerate([(out, to_out), (scores, to_scores)])]
    for copy in copies:
        copy.start()
    for copy in copies:
        copy.wait()


def per_device(nr, nc, grads, tests):
    count, own = tests.shape
    held, width = grads.shape
    quad = nr // 2
    chips = quad * nc
    half = own // 2
    share = half // quad
    span = count // GROUPS
    power = nr & (nr - 1) == 0 and nc & (nc - 1) == 0 and nr >= 4 and nc >= 2
    if not power or own * nc != width or half % (128 * quad) or count % (16 * GROUPS) or count > 128 or held % 16 or held * width > 2**23:
        return plain(grads, tests)
    bf16, f32 = jnp.bfloat16, jnp.float32
    dma = pltpu.SemaphoreType.DMA
    pairs = [(nc,), (GROUPS, nc), (quad,), (2, GROUPS), (2,), (2, chips), (chips,), (2, quad), (nc,), (chips,), (nc,), (2, quad)]
    out, scores = pl.pallas_call(
        functools.partial(kernel, nr, nc),
        out_shape=(
            jax.ShapeDtypeStruct((count, own), f32),
            jax.ShapeDtypeStruct((count, held), f32),
        ),
        in_specs=[pl.BlockSpec(memory_space=pltpu.HBM)] * 2,
        out_specs=[pl.BlockSpec(memory_space=pltpu.VMEM)] * 2,
        scratch_shapes=[
            pltpu.VMEM((2 * held, nc * half), bf16),
            pltpu.VMEM((count, own), f32),
            pltpu.VMEM((GROUPS, nc, span, half), bf16),
            pltpu.VMEM((GROUPS, nc, span, half), bf16),
            pltpu.VMEM((nc + 1, span, half), f32),
            pltpu.VMEM((quad, nc, span, share), bf16),
            pltpu.VMEM((2, nc, span, share), f32),
            pltpu.VMEM((chips, span, share), bf16),
            pltpu.VMEM((GROUPS, nc, span, half), bf16),
            pltpu.VMEM((GROUPS, span, half), bf16),
            pltpu.VMEM((2, GROUPS, 2, span, 2 * held), f32),
            pltpu.VMEM((GROUPS, span, 2 * held), f32),
            pltpu.VMEM((2, chips, 8, 128), f32),
            pltpu.VMEM((2, 8, 128), f32),
            dma((nc + 1,)),
        ]
        + [dma(shape) for shape in pairs for _ in range(2)],
        compiler_params=pltpu.CompilerParams(collective_id=0, has_side_effects=True, vmem_limit_bytes=53 * 2**20),
    )(grads, tests)
    return pl.pallas_call(
        store,
        out_shape=(
            jax.ShapeDtypeStruct((count, own), f32),
            jax.ShapeDtypeStruct((count, held), f32),
        ),
        in_specs=[pl.BlockSpec(memory_space=pltpu.VMEM)] * 2,
        out_specs=[pl.BlockSpec(memory_space=pltpu.HBM)] * 2,
        scratch_shapes=[dma((2,))],
        compiler_params=pltpu.CompilerParams(vmem_limit_bytes=2**23),
    )(out, scores)


def solution(mesh):
    placed = (P(("rows", "cols"), None), P(None, "cols"))
    return jax.shard_map(
        functools.partial(per_device, mesh.shape["rows"], mesh.shape["cols"]),
        mesh=mesh,
        in_specs=placed,
        out_specs=(P(None, "cols"), P(None, ("rows", "cols"))),
        check_vma=False,
    )
```

```python
import functools

import jax
import jax.numpy as jnp
from jax import lax
from jax.experimental import pallas as pl
from jax.experimental.pallas import tpu as pltpu
from jax.sharding import PartitionSpec as P

MESH = pl.DeviceIdType.MESH
GROUPS = 2

damping = 0.5


def plain(grads, tests):
    n_total = grads.shape[0] * lax.axis_size("rows") * lax.axis_size("cols")
    width = grads.shape[1]
    own = tests.shape[1]
    direction = lax.all_gather(tests, "cols", axis=1, tiled=True)
    norm_now = jnp.sum(direction * direction, axis=1)

    def project(d):
        return lax.dot_general(
            grads, d.astype(jnp.bfloat16), (((1,), (1,)), ((), ())), preferred_element_type=jnp.float32
        )

    partial_value = lax.dot_general(
        project(direction).astype(jnp.bfloat16), grads, (((0,), (0,)), ((), ())), preferred_element_type=jnp.float32
    )
    image = lax.psum(partial_value, ("rows", "cols")) / n_total + damping * direction
    alpha = norm_now / jnp.sum(direction * image, axis=1)
    solution = alpha[:, None] * direction
    residual = direction - alpha[:, None] * image
    norm_next = jnp.sum(residual * residual, axis=1)
    direction = residual + (norm_next / norm_now)[:, None] * direction
    proj = project(direction)
    curv = lax.psum(jnp.sum(proj * proj.astype(jnp.bfloat16).astype(jnp.float32), axis=0), ("rows", "cols"))
    curv = curv / n_total + damping * jnp.sum(direction * direction, axis=1)
    solution = solution + (norm_next / curv)[:, None] * direction
    scores = lax.dot_general(
        solution.astype(jnp.bfloat16), grads, (((1,), (1,)), ((), ())), preferred_element_type=jnp.float32
    )
    mine = lax.dynamic_slice_in_dim(solution, lax.axis_index("cols") * own, own, axis=1)
    return (mine, scores * width ** (-0.5))


def flip(value, mask):
    out, b = value, 1
    while b <= mask:
        if mask & b:
            out = out + (1 - 2 * lax.rem(lax.div(value, b), 2)) * b
        b *= 2
    return out


def kernel(
    nr, nc, grads, tests, out, scores, g, tz, tb, bk, keep, relay, late, hop, box, r, ro, px, p1s, mail, near,
    load_sem, gsend, grecv, tsend, trecv, fsend, frecv, xsend, xrecv, osend, orecv, msend, mrecv, bsend, brecv,
    csend, crecv, dsend, drecv, asend, arecv, usend, urecv, vsend, vrecv,
):
    row, col = lax.axis_index("rows"), lax.axis_index("cols")
    core, xy = lax.rem(row, 2), lax.div(row, 2)
    quad = nr // 2
    count, own = tests.shape
    held, width = grads.shape
    half = own // 2
    share = half // quad
    chips = quad * nc
    n_total = held * nr * nc
    span = count // GROUPS
    away = sorted(range(1, nc), reverse=True)
    groups = range(GROUPS)
    A, B = groups
    far = nc - 1

    def rows(a):
        return pl.ds(a * span, span)

    def at(index, size):
        return pl.ds(pl.multiple_of(index * size, size), size)

    def peer(dxy, dz):
        return {"rows": flip(xy, dxy) * 2 + core, "cols": flip(col, dz)}

    twin = {"rows": xy * 2 + 1 - core, "cols": col}
    everyone = [(dxy, dz) for dz in away + [0] for dxy in range(quad - 1, -1, -1) if dxy or dz]
    sent = []
    flying = {}

    def remote(src, dst, send, recv, device):
        copy = pltpu.make_async_remote_copy(
            src_ref=src, dst_ref=dst, send_sem=send, recv_sem=recv, device_id=device, device_id_type=MESH
        )
        copy.start()
        sent.append(copy)
        return copy

    mine = pltpu.make_async_copy(tests, tz, load_sem.at[nc])
    mine.start()
    loads = []
    for dz in range(nc):
        loads.append(
            pltpu.make_async_copy(
                grads.at[:, at(flip(col, dz) * 2 + core, half)],
                g.at[at(core, held), pl.ds(dz * half, half)],
                load_sem.at[dz],
            )
        )
        loads[-1].start()

    barrier = pltpu.get_barrier_semaphore()
    greet = [twin] + [peer(dxy, 0) for dxy in range(1, quad)] + [peer(0, dz) for dz in range(1, nc)]
    for device in greet:
        pl.semaphore_signal(barrier, inc=1, device_id=device, device_id_type=MESH)
    mine.wait()
    for a in groups:
        tb[a, 0] = tz[rows(a), at(core, half)].astype(jnp.bfloat16)
    pl.semaphore_wait(barrier, len(greet))

    here = at(xy, share)
    for dz in away:
        part = tb.at[B, 0, :, here]
        flying["quarter", dz] = remote(part, tb.at[B, dz, :, here], tsend.at[B, dz], trecv.at[B, dz], peer(0, dz))
    for dz in away:
        flying["tests", dz] = remote(tb.at[A, 0], tb.at[A, dz], tsend.at[A, dz], trecv.at[A, dz], peer(0, dz))
    for dz in range(nc):
        flying["grads", dz] = remote(
            grads.at[:, at(flip(col, dz) * 2 + 1 - core, half)],
            g.at[at(core, held), pl.ds(dz * half, half)],
            gsend.at[dz],
            grecv.at[dz],
            twin,
        )

    def across(x):
        return jnp.sum(x, axis=1, keepdims=True)

    diagonal = lax.broadcasted_iota(jnp.int32, (count, 128), 0) == lax.broadcasted_iota(jnp.int32, (count, 128), 1)
    line = lax.broadcasted_iota(jnp.int32, (8, 128), 0)

    def pack(columns):
        tile = jnp.zeros((8, 128), jnp.float32)
        for i, c in enumerate(columns):
            if c is not None:
                flat = jnp.sum(jnp.where(diagonal, jnp.broadcast_to(c, (count, 128)), 0.0), axis=0, keepdims=True)
                tile = jnp.where(line == i, jnp.broadcast_to(flat, (8, 128)), tile)
        return tile

    def unpack(tile, i):
        return across(jnp.where(diagonal, jnp.broadcast_to(tile[i : i + 1, :], (count, 128)), 0.0))

    def project(block, lo, size):
        return lax.dot_general(
            block, g[:, pl.ds(lo, size)], (((1,), (1,)), ((), ())), preferred_element_type=jnp.float32
        )

    def slot(buf, a, dz):
        return project(buf[a, dz], dz * half, half)

    def piece(buf, a, dz, dxy):
        at_xy = flip(xy, dxy)
        return project(buf[a, dz, :, at(at_xy, share)], pl.multiple_of(dz * half + at_xy * share, share), share)

    def exchange(k, a, value):
        px[k, a, 0] = value
        return remote(px.at[k, a, 0], px.at[k, a, 1], xsend.at[k, a], xrecv.at[k, a], twin)

    def post(k, tile):
        mail[k, 0] = tile
        for dxy, dz in everyone:
            j = dz * quad + dxy
            flying["mail", k, j] = remote(mail.at[k, 0], mail.at[k, j], msend.at[k, j], mrecv.at[k, j], peer(dxy, dz))

    def collect(k):
        tile = mail[k, 0]
        for j in range(1, chips):
            flying["mail", k, j].wait_recv()
            tile = tile + mail[k, j]
        return tile

    squares = across(tz[...] * tz[...])
    for dz in range(nc):
        loads[dz].wait()
        flying["grads", dz].wait_recv()
    totals = [slot(tb, a, 0) for a in groups]
    for dz in away:
        flying["quarter", dz].wait_recv()
    for dxy in range(quad - 1, 0, -1):
        part = tb.at[B, pl.ds(1, nc - 1), :, here]
        flying["spread", dxy] = remote(part, part, fsend.at[dxy], frecv.at[dxy], peer(dxy, 0))
    for dz in range(1, nc):
        totals[B] = totals[B] + piece(tb, B, dz, 0)
    for dz in range(1, nc):
        flying["tests", dz].wait_recv()
        totals[A] = totals[A] + slot(tb, A, dz)
    flying["first", A] = exchange(0, A, totals[A])
    for dxy in range(1, quad):
        flying["spread", dxy].wait_recv()
        for dz in range(1, nc):
            totals[B] = totals[B] + piece(tb, B, dz, dxy)
    flying["first", B] = exchange(0, B, totals[B])

    def arrived(k, a, name):
        flying[name, a].wait_recv()
        return px[k, a, 0] + px[k, a, 1]

    def spread(flat, a, dz):
        back = jnp.dot(flat, g[:, pl.ds(dz * half, half)], preferred_element_type=jnp.float32)
        bk[a, dz] = back.astype(jnp.bfloat16)
        return back

    p1s[A] = arrived(0, A, "first")
    flat = p1s[A].astype(jnp.bfloat16)
    for dz in away + [0]:
        back = spread(flat, A, dz)
        if dz in (0, far):
            keep[nc + dz // far] = back
        for dxy in range(quad - 1, -1, -1):
            if dxy or dz and dz < far:
                j = dz * quad + dxy
                flying["back", j] = remote(
                    bk.at[A, dz, :, at(flip(xy, dxy), share)], box.at[j], bsend.at[j], brecv.at[j], peer(dxy, dz if dz < far else 0)
                )

    p1s[B] = arrived(0, B, "first")
    flat = p1s[B].astype(jnp.bfloat16)
    for k, lo in enumerate((nc // 2, 0)):
        two = pl.ds(lo, nc // 2)
        for dz in range(lo, lo + nc // 2):
            keep[dz] = spread(flat, B, dz)
        for dxy in range(quad - 1, 0, -1):
            part = bk.at[B, two, :, at(flip(xy, dxy), share)]
            flying["side", k, dxy] = remote(
                part, relay.at[dxy, two], csend.at[k, dxy], crecv.at[k, dxy], peer(dxy, 0)
            )
    post(0, pack([jnp.concatenate([across(p1s[a] * p1s[a]) for a in groups], axis=0), squares]))

    total = keep[nc + 1, :, here]
    for dxy in range(1, quad):
        j = far * quad + dxy
        flying["back", j].wait_recv()
        total = total + box[j].astype(jnp.float32)
    hop[0] = total.astype(hop.dtype)
    j = far * quad
    flying["back", j] = remote(hop.at[0], hop.at[1], bsend.at[j], brecv.at[j], peer(0, far))

    for dz in away + [0]:
        total = keep[dz, :, here]
        for dxy in range(1, quad):
            if dz % (nc // 2) == nc // 2 - 1:
                flying["side", 1 - dz // (nc // 2), dxy].wait_recv()
            total = total + relay[dxy, dz].astype(jnp.float32)
        late[0, dz] = total.astype(late.dtype)
        if dz:
            flying["along", dz] = remote(late.at[0, dz], late.at[1, dz], dsend.at[dz], drecv.at[dz], peer(0, dz))
    tile = collect(0)
    first, rr = unpack(tile, 0), unpack(tile, 1) * (1.0 / quad)
    alpha = rr / (first * (1.0 / n_total) + damping * rr)

    def residual(a, total):
        t = tz[rows(a), at(core * quad + xy, share)]
        res = t - alpha[a * span : (a + 1) * span] * (total * (1.0 / n_total) + damping * t)
        r[a, 0, :, here] = res.astype(jnp.bfloat16)
        return res, t

    total = keep[nc, :, here]
    for j in range(1, far * quad):
        flying["back", j].wait_recv()
        total = total + box[j].astype(jnp.float32)
    flying["back", far * quad].wait_recv()
    total = total + hop[1].astype(jnp.float32)
    sums_a = residual(A, total)
    for dz in away:
        flying["up", dz] = remote(r.at[A, 0, :, here], r.at[A, dz, :, here], usend.at[dz], urecv.at[dz], peer(0, dz))
    total = late[0, 0].astype(jnp.float32)
    for dz in range(1, nc):
        flying["along", dz].wait_recv()
        total = total + late[1, dz].astype(jnp.float32)
    sums_b = residual(B, total)
    for dxy, dz in everyone:
        if dz == nc - 1 and dxy:
            continue
        j = dz * quad + dxy
        flying["res", j] = remote(r.at[B, 0, :, here], r.at[B, dz, :, here], asend.at[j], arecv.at[j], peer(dxy, dz))
    res, t = [jnp.concatenate([sums_a[i], sums_b[i]], axis=0) for i in range(2)]
    near[0] = pack([across(res * res), across(res * t)])
    flying["near"] = remote(near.at[0], near.at[1], osend.at[0], orecv.at[0], twin)

    for k, lo in enumerate((0, nc // 2)):
        for dz in range(max(lo, 1), lo + nc // 2):
            flying["up", dz].wait_recv()
        for dxy in range(quad - 1, 0, -1):
            part = r.at[A, pl.ds(lo, nc // 2), :, here]
            flying["out", k, dxy] = remote(part, part, vsend.at[k, dxy], vrecv.at[k, dxy], peer(dxy, 0))

    flying["res", far * quad].wait_recv()
    for dxy in range(quad - 1, 0, -1):
        j = far * quad + dxy
        part = r.at[B, far, :, here]
        flying["res", j] = remote(part, part, asend.at[j], arecv.at[j], peer(dxy, 0))

    p2 = jnp.zeros((count, 2 * held), jnp.float32)
    for dz in range(nc):
        for dxy in range(quad):
            if dxy and dz % (nc // 2) == 0:
                flying["out", dz // (nc // 2), dxy].wait_recv()
            if dxy or dz and dz < far:
                flying["res", dz * quad + dxy].wait_recv()
        p2 = p2 + project(jnp.concatenate([r[a, dz] for a in groups], axis=0), dz * half, half)
    for a in groups:
        px[1, a, 0] = p2[a * span : (a + 1) * span]
    flying["second"] = remote(px.at[1, :, 0], px.at[1, :, 1], xsend.at[1, 0], xrecv.at[1, 0], twin)
    flying["other"] = remote(r.at[:, 0], ro, osend.at[1], orecv.at[1], twin)
    flying["near"].wait_recv()
    tile = near[0] + near[1]
    flying["second"].wait_recv()
    p2s = [px[1, a, 0] + px[1, a, 1] for a in groups]
    moved = [jnp.concatenate([across(p2s[a] * other) for a, other in pairs], axis=0) for pairs in (
        [(a, p2s[a]) for a in groups],
        [(a, p1s[a]) for a in groups],
    )]
    post(1, tile + pack([None, None] + moved))

    tile = collect(1)
    rn, rt, ss, sp = [unpack(tile, i) for i in range(4)]
    beta = rn / rr
    curv = (ss + 2.0 * beta * sp + beta * beta * first) * (1.0 / n_total)
    curv = curv + damping * (rn + 2.0 * beta * rt + beta * beta * rr)
    step = rn / curv
    weight = alpha + step * beta
    flying["other"].wait_recv()
    for a in groups:
        w, s = weight[a * span : (a + 1) * span], step[a * span : (a + 1) * span]
        out[rows(a), at(core, half)] = w * tz[rows(a), at(core, half)] + s * r[a, 0].astype(jnp.float32)
        out[rows(a), at(1 - core, half)] = w * tz[rows(a), at(1 - core, half)] + s * ro[a].astype(jnp.float32)
        both = (w * p1s[a] + s * p2s[a]) * width ** (-0.5)
        scores[rows(a), :] = jnp.where(core == 0, both[:, :held], both[:, held:])
    for copy in sent:
        copy.wait_send()


def store(out, scores, to_out, to_scores, sem):
    copies = [pltpu.make_async_copy(src, dst, sem.at[i]) for i, (src, dst) in enumerate([(out, to_out), (scores, to_scores)])]
    for copy in copies:
        copy.start()
    for copy in copies:
        copy.wait()


def per_device(nr, nc, grads, tests):
    count, own = tests.shape
    held, width = grads.shape
    quad = nr // 2
    chips = quad * nc
    half = own // 2
    share = half // quad
    span = count // GROUPS
    power = nr & (nr - 1) == 0 and nc & (nc - 1) == 0 and nr >= 4 and nc >= 2
    if not power or own * nc != width or half % (128 * quad) or count % (16 * GROUPS) or count > 128 or held % 16 or held * width > 2**23:
        return plain(grads, tests)
    bf16, f32 = jnp.bfloat16, jnp.float32
    dma = pltpu.SemaphoreType.DMA
    pairs = [(nc,), (GROUPS, nc), (quad,), (2, GROUPS), (2,), (2, chips), (chips,), (2, quad), (nc,), (chips,), (nc,), (2, quad)]
    out, scores = pl.pallas_call(
        functools.partial(kernel, nr, nc),
        out_shape=(
            jax.ShapeDtypeStruct((count, own), f32),
            jax.ShapeDtypeStruct((count, held), f32),
        ),
        in_specs=[pl.BlockSpec(memory_space=pltpu.HBM)] * 2,
        out_specs=[pl.BlockSpec(memory_space=pltpu.VMEM)] * 2,
        scratch_shapes=[
            pltpu.VMEM((2 * held, nc * half), bf16),
            pltpu.VMEM((count, own), f32),
            pltpu.VMEM((GROUPS, nc, span, half), bf16),
            pltpu.VMEM((GROUPS, nc, span, half), bf16),
            pltpu.VMEM((nc + 2, span, half), f32),
            pltpu.VMEM((quad, nc, span, share), bf16),
            pltpu.VMEM((2, nc, span, share), bf16),
            pltpu.VMEM((2, span, share), bf16),
            pltpu.VMEM((chips, span, share), bf16),
            pltpu.VMEM((GROUPS, nc, span, half), bf16),
            pltpu.VMEM((GROUPS, span, half), bf16),
            pltpu.VMEM((2, GROUPS, 2, span, 2 * held), f32),
            pltpu.VMEM((GROUPS, span, 2 * held), f32),
            pltpu.VMEM((2, chips, 8, 128), f32),
            pltpu.VMEM((2, 8, 128), f32),
            dma((nc + 1,)),
        ]
        + [dma(shape) for shape in pairs for _ in range(2)],
        compiler_params=pltpu.CompilerParams(collective_id=0, has_side_effects=True, vmem_limit_bytes=53 * 2**20),
    )(grads, tests)
    return pl.pallas_call(
        store,
        out_shape=(
            jax.ShapeDtypeStruct((count, own), f32),
            jax.ShapeDtypeStruct((count, held), f32),
        ),
        in_specs=[pl.BlockSpec(memory_space=pltpu.VMEM)] * 2,
        out_specs=[pl.BlockSpec(memory_space=pltpu.HBM)] * 2,
        scratch_shapes=[dma((2,))],
        compiler_params=pltpu.CompilerParams(vmem_limit_bytes=2**23),
    )(out, scores)


def solution(mesh):
    placed = (P(("rows", "cols"), None), P(None, "cols"))
    return jax.shard_map(
        functools.partial(per_device, mesh.shape["rows"], mesh.shape["cols"]),
        mesh=mesh,
        in_specs=placed,
        out_specs=(P(None, "cols"), P(None, ("rows", "cols"))),
        check_vma=False,
    )
```

```python
import functools

import jax
import jax.numpy as jnp
from jax import lax
from jax.experimental import pallas as pl
from jax.experimental.pallas import tpu as pltpu
from jax.sharding import PartitionSpec as P

MESH = pl.DeviceIdType.MESH
GROUPS = 2

damping = 0.5


def plain(grads, tests):
    n_total = grads.shape[0] * lax.axis_size("rows") * lax.axis_size("cols")
    width = grads.shape[1]
    own = tests.shape[1]
    direction = lax.all_gather(tests, "cols", axis=1, tiled=True)
    norm_now = jnp.sum(direction * direction, axis=1)

    def project(d):
        return lax.dot_general(
            grads, d.astype(jnp.bfloat16), (((1,), (1,)), ((), ())), preferred_element_type=jnp.float32
        )

    partial_value = lax.dot_general(
        project(direction).astype(jnp.bfloat16), grads, (((0,), (0,)), ((), ())), preferred_element_type=jnp.float32
    )
    image = lax.psum(partial_value, ("rows", "cols")) / n_total + damping * direction
    alpha = norm_now / jnp.sum(direction * image, axis=1)
    solution = alpha[:, None] * direction
    residual = direction - alpha[:, None] * image
    norm_next = jnp.sum(residual * residual, axis=1)
    direction = residual + (norm_next / norm_now)[:, None] * direction
    proj = project(direction)
    curv = lax.psum(jnp.sum(proj * proj.astype(jnp.bfloat16).astype(jnp.float32), axis=0), ("rows", "cols"))
    curv = curv / n_total + damping * jnp.sum(direction * direction, axis=1)
    solution = solution + (norm_next / curv)[:, None] * direction
    scores = lax.dot_general(
        solution.astype(jnp.bfloat16), grads, (((1,), (1,)), ((), ())), preferred_element_type=jnp.float32
    )
    mine = lax.dynamic_slice_in_dim(solution, lax.axis_index("cols") * own, own, axis=1)
    return (mine, scores * width ** (-0.5))


def flip(value, mask):
    out, b = value, 1
    while b <= mask:
        if mask & b:
            out = out + (1 - 2 * lax.rem(lax.div(value, b), 2)) * b
        b *= 2
    return out


def kernel(
    nr, nc, grads, tests, out, scores, g, tz, tb, bk, keep, relay, late, hop, box, r, ro, px, p1s, mail, near,
    load_sem, gsend, grecv, tsend, trecv, fsend, frecv, xsend, xrecv, osend, orecv, msend, mrecv, bsend, brecv,
    csend, crecv, dsend, drecv, asend, arecv, usend, urecv, vsend, vrecv,
):
    row, col = lax.axis_index("rows"), lax.axis_index("cols")
    core, xy = lax.rem(row, 2), lax.div(row, 2)
    quad = nr // 2
    count, own = tests.shape
    held, width = grads.shape
    half = own // 2
    share = half // quad
    chips = quad * nc
    n_total = held * nr * nc
    span = count // GROUPS
    away = sorted(range(1, nc), reverse=True)
    groups = range(GROUPS)
    A, B = groups
    far = nc - 1

    def rows(a):
        return pl.ds(a * span, span)

    def at(index, size):
        return pl.ds(pl.multiple_of(index * size, size), size)

    def peer(dxy, dz):
        return {"rows": flip(xy, dxy) * 2 + core, "cols": flip(col, dz)}

    twin = {"rows": xy * 2 + 1 - core, "cols": col}
    everyone = [(dxy, dz) for dz in away[:1] + [0] + away[:0:-1] for dxy in range(quad - 1, -1, -1) if dxy or dz]
    sent = []
    flying = {}

    def remote(src, dst, send, recv, device):
        copy = pltpu.make_async_remote_copy(
            src_ref=src, dst_ref=dst, send_sem=send, recv_sem=recv, device_id=device, device_id_type=MESH
        )
        copy.start()
        sent.append(copy)
        return copy

    mine = pltpu.make_async_copy(tests, tz, load_sem.at[nc])
    mine.start()
    loads = []
    for dz in range(nc):
        loads.append(
            pltpu.make_async_copy(
                grads.at[:, at(flip(col, dz) * 2 + core, half)],
                g.at[at(core, held), pl.ds(dz * half, half)],
                load_sem.at[dz],
            )
        )
        loads[-1].start()

    barrier = pltpu.get_barrier_semaphore()
    greet = [twin] + [peer(dxy, 0) for dxy in range(1, quad)] + [peer(0, dz) for dz in range(1, nc)]
    for device in greet:
        pl.semaphore_signal(barrier, inc=1, device_id=device, device_id_type=MESH)
    mine.wait()
    for a in groups:
        tb[a, 0] = tz[rows(a), at(core, half)].astype(jnp.bfloat16)
    pl.semaphore_wait(barrier, len(greet))

    here = at(xy, share)
    for dz in away:
        part = tb.at[B, 0, :, here]
        flying["quarter", dz] = remote(part, tb.at[B, dz, :, here], tsend.at[B, dz], trecv.at[B, dz], peer(0, dz))
    for dz in away:
        flying["tests", dz] = remote(tb.at[A, 0], tb.at[A, dz], tsend.at[A, dz], trecv.at[A, dz], peer(0, dz))
    for dz in range(nc):
        flying["grads", dz] = remote(
            grads.at[:, at(flip(col, dz) * 2 + 1 - core, half)],
            g.at[at(core, held), pl.ds(dz * half, half)],
            gsend.at[dz],
            grecv.at[dz],
            twin,
        )

    def across(x):
        return jnp.sum(x, axis=1, keepdims=True)

    diagonal = lax.broadcasted_iota(jnp.int32, (count, 128), 0) == lax.broadcasted_iota(jnp.int32, (count, 128), 1)
    line = lax.broadcasted_iota(jnp.int32, (8, 128), 0)

    def pack(columns):
        tile = jnp.zeros((8, 128), jnp.float32)
        for i, c in enumerate(columns):
            if c is not None:
                flat = jnp.sum(jnp.where(diagonal, jnp.broadcast_to(c, (count, 128)), 0.0), axis=0, keepdims=True)
                tile = jnp.where(line == i, jnp.broadcast_to(flat, (8, 128)), tile)
        return tile

    def unpack(tile, i):
        return across(jnp.where(diagonal, jnp.broadcast_to(tile[i : i + 1, :], (count, 128)), 0.0))

    def project(block, lo, size):
        return lax.dot_general(
            block, g[:, pl.ds(lo, size)], (((1,), (1,)), ((), ())), preferred_element_type=jnp.float32
        )

    def slot(buf, a, dz):
        return project(buf[a, dz], dz * half, half)

    def piece(buf, a, dz, dxy):
        at_xy = flip(xy, dxy)
        return project(buf[a, dz, :, at(at_xy, share)], pl.multiple_of(dz * half + at_xy * share, share), share)

    def exchange(k, a, value):
        px[k, a, 0] = value
        return remote(px.at[k, a, 0], px.at[k, a, 1], xsend.at[k, a], xrecv.at[k, a], twin)

    def post(k, tile):
        mail[k, 0] = tile
        for dxy, dz in everyone:
            j = dz * quad + dxy
            flying["mail", k, j] = remote(mail.at[k, 0], mail.at[k, j], msend.at[k, j], mrecv.at[k, j], peer(dxy, dz))

    def collect(k):
        tile = mail[k, 0]
        for j in range(1, chips):
            flying["mail", k, j].wait_recv()
            tile = tile + mail[k, j]
        return tile

    squares = pack([None, across(tz[...] * tz[...])])
    for dz in range(nc):
        loads[dz].wait()
        flying["grads", dz].wait_recv()
    totals = [slot(tb, a, 0) for a in groups]
    for dz in away:
        flying["quarter", dz].wait_recv()
    for dxy in range(quad - 1, 0, -1):
        part = tb.at[B, pl.ds(1, nc - 1), :, here]
        flying["spread", dxy] = remote(part, part, fsend.at[dxy], frecv.at[dxy], peer(dxy, 0))
    for dz in range(1, nc):
        totals[B] = totals[B] + piece(tb, B, dz, 0)
    for dz in range(1, nc):
        flying["tests", dz].wait_recv()
        totals[A] = totals[A] + slot(tb, A, dz)
    flying["first", A] = exchange(0, A, totals[A])
    for dxy in range(1, quad):
        flying["spread", dxy].wait_recv()
        for dz in range(1, nc):
            totals[B] = totals[B] + piece(tb, B, dz, dxy)
    flying["first", B] = exchange(0, B, totals[B])

    def arrived(k, a, name):
        flying[name, a].wait_recv()
        return px[k, a, 0] + px[k, a, 1]

    def spread(flat, a, dz):
        back = jnp.dot(flat, g[:, pl.ds(dz * half, half)], preferred_element_type=jnp.float32)
        bk[a, dz] = back.astype(jnp.bfloat16)
        return back

    p1s[A] = arrived(0, A, "first")
    flat = p1s[A].astype(jnp.bfloat16)
    for dz in away + [0]:
        back = spread(flat, A, dz)
        if dz in (0, far):
            keep[nc + dz // far] = back
        for dxy in range(quad - 1, -1, -1):
            if dxy or dz and dz < far:
                j = dz * quad + dxy
                flying["back", j] = remote(
                    bk.at[A, dz, :, at(flip(xy, dxy), share)], box.at[j], bsend.at[j], brecv.at[j], peer(dxy, dz if dz < far else 0)
                )

    p1s[B] = arrived(0, B, "first")
    flat = p1s[B].astype(jnp.bfloat16)
    for k, lo in enumerate((nc // 2, 0)):
        two = pl.ds(lo, nc // 2)
        for dz in range(lo, lo + nc // 2):
            keep[dz] = spread(flat, B, dz)
        for dxy in range(quad - 1, 0, -1):
            part = bk.at[B, two, :, at(flip(xy, dxy), share)]
            flying["side", k, dxy] = remote(
                part, relay.at[dxy, two], csend.at[k, dxy], crecv.at[k, dxy], peer(dxy, 0)
            )

    total = keep[nc + 1, :, here]
    for dxy in range(1, quad):
        j = far * quad + dxy
        flying["back", j].wait_recv()
        total = total + box[j].astype(jnp.float32)
    hop[0] = total.astype(hop.dtype)
    j = far * quad
    flying["back", j] = remote(hop.at[0], hop.at[1], bsend.at[j], brecv.at[j], peer(0, far))

    post(0, squares + pack([jnp.concatenate([across(p1s[a] * p1s[a]) for a in groups], axis=0)]))
    for dz in away + [0]:
        total = keep[dz, :, here]
        for dxy in range(1, quad):
            if dz % (nc // 2) == nc // 2 - 1:
                flying["side", 1 - dz // (nc // 2), dxy].wait_recv()
            total = total + relay[dxy, dz].astype(jnp.float32)
        late[0, dz] = total.astype(late.dtype)
        if dz:
            flying["along", dz] = remote(late.at[0, dz], late.at[1, dz], dsend.at[dz], drecv.at[dz], peer(0, dz))
    tile = collect(0)
    first, rr = unpack(tile, 0), unpack(tile, 1) * (1.0 / quad)
    alpha = rr / (first * (1.0 / n_total) + damping * rr)

    def residual(a, total):
        t = tz[rows(a), at(core * quad + xy, share)]
        res = t - alpha[a * span : (a + 1) * span] * (total * (1.0 / n_total) + damping * t)
        r[a, 0, :, here] = res.astype(jnp.bfloat16)
        return res, t

    total = keep[nc, :, here]
    for j in range(1, far * quad):
        flying["back", j].wait_recv()
        total = total + box[j].astype(jnp.float32)
    flying["back", far * quad].wait_recv()
    total = total + hop[1].astype(jnp.float32)
    sums_a = residual(A, total)
    for dz in away:
        flying["up", dz] = remote(r.at[A, 0, :, here], r.at[A, dz, :, here], usend.at[dz], urecv.at[dz], peer(0, dz))
    total = late[0, 0].astype(jnp.float32)
    for dz in range(1, nc):
        flying["along", dz].wait_recv()
        total = total + late[1, dz].astype(jnp.float32)
    sums_b = residual(B, total)
    for dxy, dz in everyone:
        if dz == nc - 1 and dxy:
            continue
        j = dz * quad + dxy
        flying["res", j] = remote(r.at[B, 0, :, here], r.at[B, dz, :, here], asend.at[j], arecv.at[j], peer(dxy, dz))
    res, t = [jnp.concatenate([sums_a[i], sums_b[i]], axis=0) for i in range(2)]
    near[0] = pack([across(res * res), across(res * t)])
    flying["near"] = remote(near.at[0], near.at[1], osend.at[0], orecv.at[0], twin)

    for k, lo in enumerate((0, nc // 2)):
        for dz in range(max(lo, 1), lo + nc // 2):
            flying["up", dz].wait_recv()
        for dxy in range(quad - 1, 0, -1):
            part = r.at[A, pl.ds(lo, nc // 2), :, here]
            flying["out", k, dxy] = remote(part, part, vsend.at[k, dxy], vrecv.at[k, dxy], peer(dxy, 0))

    flying["res", far * quad].wait_recv()
    for dxy in range(quad - 1, 0, -1):
        j = far * quad + dxy
        part = r.at[B, far, :, here]
        flying["res", j] = remote(part, part, asend.at[j], arecv.at[j], peer(dxy, 0))

    def joint(dz, dxy):
        index = flip(xy, dxy)
        block = jnp.concatenate([r[a, dz, :, at(index, share)] for a in groups], axis=0)
        return project(block, pl.multiple_of(dz * half + index * share, share), share)

    p2 = jnp.zeros((count, 2 * held), jnp.float32)
    for dz in range(nc):
        if dz == far:
            p2 = p2 + joint(dz, 0)
        for dxy in range(quad):
            if dxy and (dz % (nc // 2) == 0):
                flying["out", dz // (nc // 2), dxy].wait_recv()
            if dxy or dz and dz < far:
                flying["res", dz * quad + dxy].wait_recv()
            if dz == far and dxy:
                p2 = p2 + joint(dz, dxy)
        if dz < far:
            p2 = p2 + project(jnp.concatenate([r[a, dz] for a in groups], axis=0), dz * half, half)
    for a in groups:
        px[1, a, 0] = p2[a * span : (a + 1) * span]
    flying["second"] = remote(px.at[1, :, 0], px.at[1, :, 1], xsend.at[1, 0], xrecv.at[1, 0], twin)
    flying["near"].wait_recv()
    tile = near[0] + near[1]
    flying["second"].wait_recv()
    p2s = [px[1, a, 0] + px[1, a, 1] for a in groups]
    moved = [jnp.concatenate([across(p2s[a] * other) for a, other in pairs], axis=0) for pairs in (
        [(a, p2s[a]) for a in groups],
        [(a, p1s[a]) for a in groups],
    )]
    earlier = list(sent)
    post(1, tile + pack([None, None] + moved))
    flying["other"] = remote(r.at[:, 0], ro, osend.at[1], orecv.at[1], twin)
    for copy in earlier:
        copy.wait_send()

    tile = collect(1)
    rn, rt, ss, sp = [unpack(tile, i) for i in range(4)]
    beta = rn / rr
    curv = (ss + 2.0 * beta * sp + beta * beta * first) * (1.0 / n_total)
    curv = curv + damping * (rn + 2.0 * beta * rt + beta * beta * rr)
    step = rn / curv
    weight = alpha + step * beta
    flying["other"].wait_recv()
    for a in groups:
        w, s = weight[a * span : (a + 1) * span], step[a * span : (a + 1) * span]
        out[rows(a), at(core, half)] = w * tz[rows(a), at(core, half)] + s * r[a, 0].astype(jnp.float32)
        out[rows(a), at(1 - core, half)] = w * tz[rows(a), at(1 - core, half)] + s * ro[a].astype(jnp.float32)
        both = (w * p1s[a] + s * p2s[a]) * width ** (-0.5)
        scores[rows(a), :] = jnp.where(core == 0, both[:, :held], both[:, held:])
    for copy in sent[len(earlier) :]:
        copy.wait_send()


def store(out, scores, to_out, to_scores, sem):
    copies = [pltpu.make_async_copy(src, dst, sem.at[i]) for i, (src, dst) in enumerate([(out, to_out), (scores, to_scores)])]
    for copy in copies:
        copy.start()
    for copy in copies:
        copy.wait()


def per_device(nr, nc, grads, tests):
    count, own = tests.shape
    held, width = grads.shape
    quad = nr // 2
    chips = quad * nc
    half = own // 2
    share = half // quad
    span = count // GROUPS
    power = nr & (nr - 1) == 0 and nc & (nc - 1) == 0 and nr >= 4 and nc >= 2
    if not power or own * nc != width or half % (128 * quad) or count % (16 * GROUPS) or count > 128 or held % 16 or held * width > 2**23:
        return plain(grads, tests)
    bf16, f32 = jnp.bfloat16, jnp.float32
    dma = pltpu.SemaphoreType.DMA
    pairs = [(nc,), (GROUPS, nc), (quad,), (2, GROUPS), (2,), (2, chips), (chips,), (2, quad), (nc,), (chips,), (nc,), (2, quad)]
    out, scores = pl.pallas_call(
        functools.partial(kernel, nr, nc),
        out_shape=(
            jax.ShapeDtypeStruct((count, own), f32),
            jax.ShapeDtypeStruct((count, held), f32),
        ),
        in_specs=[pl.BlockSpec(memory_space=pltpu.HBM)] * 2,
        out_specs=[pl.BlockSpec(memory_space=pltpu.VMEM)] * 2,
        scratch_shapes=[
            pltpu.VMEM((2 * held, nc * half), bf16),
            pltpu.VMEM((count, own), f32),
            pltpu.VMEM((GROUPS, nc, span, half), bf16),
            pltpu.VMEM((GROUPS, nc, span, half), bf16),
            pltpu.VMEM((nc + 2, span, half), f32),
            pltpu.VMEM((quad, nc, span, share), bf16),
            pltpu.VMEM((2, nc, span, share), bf16),
            pltpu.VMEM((2, span, share), bf16),
            pltpu.VMEM((chips, span, share), bf16),
            pltpu.VMEM((GROUPS, nc, span, half), bf16),
            pltpu.VMEM((GROUPS, span, half), bf16),
            pltpu.VMEM((2, GROUPS, 2, span, 2 * held), f32),
            pltpu.VMEM((GROUPS, span, 2 * held), f32),
            pltpu.VMEM((2, chips, 8, 128), f32),
            pltpu.VMEM((2, 8, 128), f32),
            dma((nc + 1,)),
        ]
        + [dma(shape) for shape in pairs for _ in range(2)],
        compiler_params=pltpu.CompilerParams(collective_id=0, has_side_effects=True, vmem_limit_bytes=53 * 2**20),
    )(grads, tests)
    return pl.pallas_call(
        store,
        out_shape=(
            jax.ShapeDtypeStruct((count, own), f32),
            jax.ShapeDtypeStruct((count, held), f32),
        ),
        in_specs=[pl.BlockSpec(memory_space=pltpu.VMEM)] * 2,
        out_specs=[pl.BlockSpec(memory_space=pltpu.HBM)] * 2,
        scratch_shapes=[dma((2,))],
        compiler_params=pltpu.CompilerParams(vmem_limit_bytes=2**23),
    )(out, scores)


def solution(mesh):
    placed = (P(("rows", "cols"), None), P(None, "cols"))
    return jax.shard_map(
        functools.partial(per_device, mesh.shape["rows"], mesh.shape["cols"]),
        mesh=mesh,
        in_specs=placed,
        out_specs=(P(None, "cols"), P(None, ("rows", "cols"))),
        check_vma=False,
    )
```
